32 devices in a mesh: groups: 2 (over x), blk: 16 (over z, y, core).
Axes of the slice: x: 2, y: 2, z: 4, core: 2. Of those that a mesh axis runs over, the one named last changes fastest.
Arguments:
- query_inputs: bfloat16 [8192, 4096], P(('groups', 'blk')), parts along dimension 0, may hold values from -6 to 6
- query_grads: bfloat16 [8192, 4096], P(('groups', 'blk')), parts along dimension 0, may hold values from -6 to 6
- proj_in: bfloat16 [4096, 64], replicated, may hold values from -0.09375 to 0.09375
- proj_out: bfloat16 [4096, 64], replicated, may hold values from -0.09375 to 0.09375
- train_rows: bfloat16 [8192, 4096], P(('groups', 'blk')), parts along dimension 0, may hold values from -0.09375 to 0.09375
- token_owner: int32 [8192, 1], P(('groups', 'blk')), parts along dimension 0, may hold values from 0 to 15; in each aligned block of 256 rows (0 to 255, 256 to 511, ...) at most 64 rows name the same one
- token_slot: int32 [8192], P(('groups', 'blk')), parts along dimension 0, may hold values from 0 to 31
Outputs:
- influence: bfloat16 [12, 32, 8192], P(None, None, ('groups', 'blk')), parts along dimension 2
The draws below stay inside these ranges and needn't reach their ends.
There are 2 independent parts, one for each index of `groups`. The reference program is written for one: setup_inputs(seed, part) draws one part's arguments, and reference() takes and returns one part's arrays. A program takes and returns all parts, laid end to end along the dimension named above; an argument that names none is the same for every part. Nothing has to cross between parts.
Inputs may be any that keep to these rules, and one draw needn't show every extreme that they name: `token_owner`: within the tokens of one device no owner is named by more than 64 tokens, a bound that some block reaches.
All inputs are finite; a program needn't handle non-finite values. Where the reference program divides by a largest or mean magnitude, that divisor is 1e-20 or more.
Results may differ from the reference program's by a relative error of at most 0.0069.
Values may be sent and summed in bfloat16 or wider, within the bound.
A program may use at most 64 MiB of HBM per device.

```python
import math
import jax
import jax.numpy as jnp
import numpy as np
from jax import lax

D = 4096
R = 64
TOK_DEV = 256
DOC_DEV = 32
TR_DEV = 256
STOPS = 12
NEWTON_STEPS = 6
LEAD = 5
OWNERS = 16
CAP = 64
TOKENS = 4096
TRAIN = 4096


def place_ends(array, stream_key, least, high):
    spot = [jax.random.randint(jax.random.fold_in(stream_key, axis), (), 0, length) for axis, length in enumerate(array.shape)]
    main_axis = array.shape.index(max(array.shape))
    beside = spot[:main_axis] + [(spot[main_axis] + 1) % array.shape[main_axis]] + spot[main_axis + 1:]
    return array.at[tuple(spot)].set(least).at[tuple(beside)].set(high)


def level_of(key, dims, cuts, low, top_value):
    def one(position, blocks):
        draws = jax.random.uniform(jax.random.fold_in(jax.random.fold_in(key, 6), position), (blocks,), jnp.float32, low / len(cuts), top_value / len(cuts))
        return jnp.repeat(jnp.exp(draws), dims[position] // blocks).reshape((-1,) + (1,) * (len(dims) - position - 1))

    factor_of = one(*cuts[0])
    for cut in cuts[1:]:
        factor_of = factor_of * one(*cut)
    return factor_of


def deal_out(stream_key, own, number, rows, count, top, limit, skew):
    ranking = jax.random.permutation(stream_key, count)
    crowded, common = load_shares(count, rows * top, limit, skew, True), load_shares(count, rows * top, limit, skew, False)
    places = jnp.arange(count)

    def named(sizes, offset_by):
        used = int((sizes > 0).sum())
        fixed = max(1, used // 4)
        passed = fixed + (places - fixed + offset_by * (used - fixed)) % max(1, count - fixed)
        return jnp.zeros((count,), jnp.int32).at[ranking[jnp.where(places < fixed, places, passed)]].set(jnp.asarray(sizes, jnp.int32))

    sizes = jnp.where(number % 4 == 0, named(crowded, number // 4), named(common, number - number // 4 - 1))
    mixed = jax.random.permutation(jax.random.fold_in(own, 3), count)
    giver, receiver = mixed[0:count // 2 * 2:2], mixed[1:count // 2 * 2:2]
    slack = jnp.minimum(sizes[giver] - 1, limit - sizes[receiver]) // 2
    slack = jnp.where((giver == ranking[0]) | (receiver == ranking[0]) | (sizes[receiver] == 0), 0, jnp.maximum(slack, 0))
    passed = jax.random.randint(jax.random.fold_in(own, 4), (count // 2,), 0, 1 << 20) % (slack + 1)
    sizes = sizes.at[giver].add(-passed).at[receiver].add(passed)
    labels = jnp.searchsorted(jnp.cumsum(sizes), jnp.arange(rows * top), side="right").astype(jnp.int32)
    table = labels.reshape(top, rows).T
    table = table[jax.random.permutation(jax.random.fold_in(own, 1), rows)]
    offset_by = jax.random.randint(jax.random.fold_in(own, 2), (rows, 1), 0, top)
    return jnp.take_along_axis(table, (jnp.arange(top)[None, :] + offset_by) % top, axis=1)


def load_shares(amount, total, reach, lean, full):
    portions = [(1 << 20) // math.isqrt(standing ** lean) + 1 for standing in range(1, amount + 1)]
    largest = reach if full else min(reach, max(-(-total // amount), total * portions[0] // sum(portions)))
    least = 1 if total - largest >= amount - 1 else 0
    holding, spare = [largest] + [least] * (amount - 1), total - largest - least * (amount - 1)
    while spare > 0:
        candidates = [i for i in range(1, amount) if holding[i] < largest] or [i for i in range(1, amount) if holding[i] < reach]
        mass, left = sum([portions[i] for i in candidates]), spare
        for i in candidates:
            extra = min(reach - holding[i], max(1, left * portions[i] // mass), spare)
            holding[i] = holding[i] + extra
            spare = spare - extra
    return np.array(holding)


def bell_draw(key, extent, deviation, bound, cuts=(), held_as=jnp.bfloat16):
    drawn = deviation * jax.random.normal(key, extent, jnp.float32)
    if cuts:
        drawn = drawn * level_of(key, extent, cuts, -0.22, 0.18)
    return jnp.clip(drawn, -bound, bound).astype(held_as)


def setup_inputs(seed: int = 0, part: int = 0) -> dict:
    seeds = jax.random.split(jax.random.key(seed), 8)
    part_keys = jax.random.split(jax.random.fold_in(seeds[7], part), 8)
    query_inputs = bell_draw(part_keys[0], (TOKENS, D), 1.0, 6.0, ((0, 16),))
    query_grads = bell_draw(part_keys[1], (TOKENS, D), 1.0, 6.0, ((0, 16),))
    proj_in = bell_draw(seeds[2], (D, R), D ** -0.5, 0.09375)
    proj_out = bell_draw(seeds[3], (D, R), D ** -0.5, 0.09375)
    train_rows = bell_draw(part_keys[4], (TRAIN, R * R), (R * R) ** -0.5, 0.09375, ((0, 16),))
    token_owner_keys = jax.random.split(jax.random.fold_in(part_keys[5], 1), TOKENS // TOK_DEV)
    token_owner_turns = jax.random.permutation(jax.random.fold_in(part_keys[5], 3), TOKENS // TOK_DEV)
    token_owner = jax.vmap(lambda own, number: deal_out(jax.random.fold_in(part_keys[5], 2), own, number, TOK_DEV, OWNERS, 1, CAP, 2))(token_owner_keys, token_owner_turns).reshape((TOKENS, 1))
    token_slot = place_ends(jax.random.randint(part_keys[6], (TOKENS,), 0, DOC_DEV), jax.random.fold_in(part_keys[6], 1), 0, DOC_DEV - 1).astype(jnp.int32)
    return {"query_inputs": query_inputs, "query_grads": query_grads, "proj_in": proj_in, "proj_out": proj_out, "train_rows": train_rows, "token_owner": token_owner, "token_slot": token_slot}


HIGHEST_PRECISION = lax.Precision.HIGHEST


def inverse_factor(gram_sum, counts):
    width_low = gram_sum.shape[1]
    identity_mat = jnp.eye(width_low, dtype=jnp.float32)
    damped = gram_sum / (counts[:, None, None] + 1.0) + identity_mat[None]
    row_bound = jnp.max(jnp.sum(jnp.abs(damped), axis=2), axis=1)
    approx = identity_mat[None] / row_bound[:, None, None]
    for iteration in range(NEWTON_STEPS):
        product = jnp.einsum("dab,dbc->dac", damped, approx, precision=HIGHEST_PRECISION)
        approx = jnp.einsum("dab,dbc->dac", approx, 2.0 * identity_mat[None] - product, precision=HIGHEST_PRECISION)
    return approx


def reference(query_inputs, query_grads, proj_in, proj_out, train_rows, token_owner, token_slot):
    grads_low = jnp.dot(query_grads, proj_out, preferred_element_type=jnp.float32).astype(jnp.bfloat16)
    inputs_low = jnp.dot(query_inputs, proj_in, preferred_element_type=jnp.float32).astype(jnp.bfloat16)
    doc_ids = (token_owner[:, 0] * DOC_DEV + token_slot).astype(jnp.int32)
    doc_total = OWNERS * DOC_DEV

    def accumulate(carried, index):
        grad_sum, input_sum, count_sum = carried
        start = (index * TOK_DEV).astype(jnp.int32)
        grads_part = lax.dynamic_slice_in_dim(grads_low, start, TOK_DEV, 0).astype(jnp.float32)
        inputs_part = lax.dynamic_slice_in_dim(inputs_low, start, TOK_DEV, 0).astype(jnp.float32)
        ids_part = lax.dynamic_slice_in_dim(doc_ids, start, TOK_DEV, 0)
        joined = jnp.concatenate([grads_part, inputs_part], axis=1)
        grad_terms = grads_part[:, :, None] * joined[:, None, :]
        input_terms = inputs_part[:, :, None] * inputs_part[:, None, :]
        grad_sum = grad_sum.at[ids_part].add(grad_terms)
        input_sum = input_sum.at[ids_part].add(input_terms)
        count_sum = count_sum.at[ids_part].add(jnp.ones((TOK_DEV,), jnp.float32))
        return (grad_sum, input_sum, count_sum), None

    start_sums = (jnp.zeros((doc_total, R, 2 * R), jnp.float32), jnp.zeros((doc_total, R, R), jnp.float32), jnp.zeros((doc_total,), jnp.float32))
    sums_done, unused = lax.scan(accumulate, start_sums, jnp.arange(OWNERS, dtype=jnp.int32))
    grad_sum, input_sum, count_sum = sums_done
    outer_b = grad_sum[:, :, :R]
    doc_grad = grad_sum[:, :, R:]
    inv_a = inverse_factor(input_sum, count_sum)
    inv_b = inverse_factor(outer_b, count_sum)
    tilted = jnp.einsum("dab,dbc->dac", inv_b, doc_grad, precision=HIGHEST_PRECISION)
    tilted = jnp.einsum("dab,dbc->dac", tilted, inv_a, precision=HIGHEST_PRECISION)
    queries = tilted.reshape(OWNERS, DOC_DEV, R * R).astype(jnp.bfloat16)
    train_blocks = train_rows.reshape(OWNERS, TR_DEV, R * R)
    offsets = jnp.arange(STOPS, dtype=jnp.int32)

    def one_device(index):
        sources = (index - offsets + LEAD) % OWNERS
        visiting = queries[sources].astype(jnp.float32)
        resident = train_blocks[index].astype(jnp.float32)
        return jnp.einsum("skf,tf->skt", visiting, resident).astype(jnp.bfloat16)

    tile_rows = lax.map(one_device, jnp.arange(OWNERS, dtype=jnp.int32))
    return jnp.transpose(tile_rows, (1, 2, 0, 3)).reshape(STOPS, DOC_DEV, OWNERS * TR_DEV)
```

```python
import functools

import jax
import jax.numpy as jnp
from jax import lax
from jax.experimental import pallas as pl
from jax.experimental.pallas import tpu as pltpu
from jax.sharding import PartitionSpec as P

DOC_DEV = 32
STOPS = 12
NEWTON_STEPS = 6
LEAD = 5
LANES = 128
DOC_GROUP = 4
MESH = pl.DeviceIdType.MESH
VMEM_SPEC = pl.BlockSpec(memory_space=pltpu.VMEM)
F32 = jnp.float32
BF16 = jnp.bfloat16
CONTRACT_LAST = (((1,), (1,)), ((), ()))


def matmul(left, right):
    return jnp.dot(left, right, preferred_element_type=F32)


def halves(value):
    high = value.astype(BF16)
    return high, (value - high.astype(F32)).astype(BF16)


def split_matmul(left, right):
    left_high, left_low = left
    right_high, right_low = right
    joined = matmul(
        jnp.concatenate([left_high, left_low], axis=1),
        jnp.concatenate([right_high, right_high], axis=0),
    )
    return joined + matmul(left_high, right_low)


def dispatch_kernel(owners, capacity, x_in, x_grad, p_in, p_out, owner_col, owner_row, slot_row,
                    recv_rows, recv_slot, low, send_rows, send_slot,
                    rows_sent, rows_here, slot_sent, slot_here):
    me = lax.axis_index("blk")
    barrier = pltpu.get_barrier_semaphore()

    @pl.loop(1, owners)
    def _(ahead):
        pl.semaphore_signal(
            barrier, inc=1, device_id={"blk": lax.rem(me + ahead, owners)}, device_id_type=MESH
        )

    count = x_in.shape[0]
    width = p_in.shape[1]
    low[:, :width] = matmul(x_grad[...], p_out[...]).astype(BF16)
    low[:, width:] = matmul(x_in[...], p_in[...]).astype(BF16)
    token = lax.broadcasted_iota(jnp.int32, (count, count), 0)
    other = lax.broadcasted_iota(jnp.int32, (count, count), 1)
    same = (owner_col[...] == owner_row[...]) & (token < other)
    rank = jnp.sum(jnp.where(same, 1.0, 0.0), axis=0, keepdims=True).astype(jnp.int32)
    position = owner_row[...] * capacity + rank
    place = lax.broadcasted_iota(jnp.int32, (owners * capacity, count), 0)
    placed = jnp.where(place == position, 1.0, 0.0).astype(BF16)
    send_rows[...] = matmul(placed, low[...]).astype(BF16).reshape(send_rows.shape)
    owner_id = lax.broadcasted_iota(jnp.int32, (owners, count), 0)
    coded = jnp.where(owner_id == owner_row[...], slot_row[...] + 1, 0).astype(F32).astype(BF16)
    lane = lax.broadcasted_iota(jnp.int32, (LANES, count), 0)
    shift = lax.rem(me, LANES // capacity) * capacity
    spread = jnp.where(lane == rank + shift, 1.0, 0.0).astype(BF16)
    codes = lax.dot_general(coded, spread, CONTRACT_LAST, preferred_element_type=F32)
    codes = codes.astype(jnp.int32)
    for owner in range(owners):
        send_slot[owner] = codes[owner:owner + 1]
    pl.semaphore_wait(barrier, owners - 1)

    def copies(target, source, sem):
        to = {"blk": target}
        return (
            pltpu.make_async_remote_copy(
                src_ref=send_rows.at[target], dst_ref=recv_rows.at[source],
                send_sem=rows_sent.at[target], recv_sem=rows_here.at[sem],
                device_id=to, device_id_type=MESH),
            pltpu.make_async_remote_copy(
                src_ref=send_slot.at[target], dst_ref=recv_slot.at[source],
                send_sem=slot_sent.at[target], recv_sem=slot_here.at[sem],
                device_id=to, device_id_type=MESH),
        )

    @pl.loop(1, owners)
    def _(ahead):
        for copy in copies(lax.rem(me + ahead, owners), me, me):
            copy.start()

    recv_rows[me] = send_rows[me]
    recv_slot[me] = send_slot[me]

    @pl.loop(1, owners)
    def _(ahead):
        source = lax.rem(me + ahead, owners)
        for copy in copies(source, source, source):
            copy.wait_recv()

    @pl.loop(1, owners)
    def _(ahead):
        for copy in copies(lax.rem(me + ahead, owners), me, me):
            copy.wait_send()


def dispatch(x_in, x_grad, p_in, p_out, owner_col, owner_row, slot_row):
    owners = lax.axis_size("blk")
    count, width = x_in.shape[0], p_in.shape[1]
    capacity = 4 * count // owners
    rows = (owners, capacity, 2 * width)
    slots = (owners, 1, LANES)
    return pl.pallas_call(
        functools.partial(dispatch_kernel, owners, capacity),
        out_shape=(jax.ShapeDtypeStruct(rows, BF16), jax.ShapeDtypeStruct(slots, jnp.int32)),
        in_specs=[VMEM_SPEC] * 7,
        out_specs=(VMEM_SPEC, VMEM_SPEC),
        scratch_shapes=[
            pltpu.VMEM((count, 2 * width), BF16),
            pltpu.VMEM(rows, BF16),
            pltpu.VMEM(slots, jnp.int32),
        ] + [pltpu.SemaphoreType.DMA((owners,))] * 4,
        compiler_params=pltpu.CompilerParams(collective_id=0, has_side_effects=True),
        name="dispatch",
    )(x_in, x_grad, p_in, p_out, owner_col, owner_row, slot_row)


def queries_kernel(recv_rows, recv_slot, out, turned, codes, flat):
    owners, capacity, full = recv_rows.shape
    width = full // 2
    total = owners * capacity
    group = LANES // capacity
    rows = recv_rows[...].reshape(total, full)
    for part in range(total // LANES):
        span = slice(part * LANES, (part + 1) * LANES)
        turned[:, span] = rows[span].T
        code = recv_slot[part * group]
        for source in range(part * group + 1, (part + 1) * group):
            code = code + recv_slot[source]
        codes[:, span] = code
    row = lax.broadcasted_iota(jnp.int32, (full, full), 0)
    col = lax.broadcasted_iota(jnp.int32, (full, full), 1)
    upper_row = row < width
    diagonal = upper_row == (col < width)
    corner = upper_row & (col >= width)
    identity_mat = jnp.where(row == col, 1.0, 0.0)
    upper = lax.broadcasted_iota(jnp.int32, (full, 1), 0) < width

    @pl.loop(0, DOC_DEV // DOC_GROUP)
    def _(step):
        docs = range(DOC_GROUP)
        code = codes[...]
        counts, masked = [], []
        for doc in docs:
            hot = jnp.where(code == step * DOC_GROUP + doc + 1, 1.0, 0.0)
            counts.append(jnp.sum(hot, axis=1, keepdims=True))
            masked.append(turned[...] * hot.astype(BF16))
        grams = matmul(jnp.concatenate(masked, axis=0), rows)
        grams = [grams[doc * full:(doc + 1) * full] for doc in docs]
        powers, approx = [], []
        for doc in docs:
            damped = jnp.where(diagonal, grams[doc] / (counts[doc] + 1.0), 0.0) + identity_mat
            sums = jnp.sum(jnp.abs(damped), axis=1, keepdims=True)
            bound = jnp.where(
                upper,
                jnp.max(sums[:width], axis=0, keepdims=True),
                jnp.max(sums[width:], axis=0, keepdims=True),
            )
            scale = 1.0 / bound
            residual = identity_mat - damped * scale
            approx.append((identity_mat + residual) * scale)
            parts = halves(residual)
            powers.append(split_matmul(parts, parts))
        for level in range(NEWTON_STEPS - 2):
            for doc in docs:
                power = halves(powers[doc])
                inverse = halves(approx[doc])
                both = tuple(
                    jnp.concatenate([p, x], axis=1) for p, x in zip(power, inverse)
                )
                product = split_matmul(power, both)
                powers[doc] = product[:, :full]
                approx[doc] = approx[doc] + product[:, full:]
        for doc in docs:
            inverse = approx[doc] + split_matmul(halves(powers[doc]), halves(approx[doc]))
            mixed = jnp.where(corner, grams[doc], 0.0)
            tilted = split_matmul(halves(inverse[:width]), halves(mixed))
            right = inverse[width:]
            right = right + pltpu.roll(right, width, 1)
            right = jnp.concatenate([jnp.zeros_like(right), right], axis=0)
            tilted = split_matmul(halves(tilted), halves(right))
            start = pl.multiple_of((step * DOC_GROUP + doc) * width, width)
            flat[pl.ds(start, width), :] = tilted

    left = lax.broadcasted_iota(jnp.int32, (DOC_DEV, full), 1) < width
    for pair in range(width // 2):
        even = flat[pl.ds(2 * pair, DOC_DEV, stride=width), :]
        odd = flat[pl.ds(2 * pair + 1, DOC_DEV, stride=width), :]
        out[:, pair * full:(pair + 1) * full] = jnp.where(left, even, odd).astype(BF16)


def make_queries(recv_rows, recv_slot):
    owners, capacity, full = recv_rows.shape
    width = full // 2
    total = owners * capacity
    return pl.pallas_call(
        queries_kernel,
        out_shape=jax.ShapeDtypeStruct((DOC_DEV, width * width), BF16),
        in_specs=[VMEM_SPEC] * 2,
        out_specs=VMEM_SPEC,
        scratch_shapes=[
            pltpu.VMEM((full, total), BF16),
            pltpu.VMEM((1, total), jnp.int32),
            pltpu.VMEM((DOC_DEV * width, full), F32),
        ],
        name="queries",
    )(recv_rows, recv_slot)


def score_into(out, index, block, train):
    out[index] = lax.dot_general(
        block[...], train[...], CONTRACT_LAST, preferred_element_type=F32
    ).astype(BF16)


def window_kernel(owners, queries, train, out, held, sent, here):
    me = lax.axis_index("blk")
    barrier = pltpu.get_barrier_semaphore()

    def peer(stop):
        return lax.rem(me + stop - LEAD + owners, owners)

    def source(stop):
        return lax.rem(me - stop + LEAD + owners, owners)

    def copy(stop):
        return pltpu.make_async_remote_copy(
            src_ref=queries, dst_ref=held.at[stop], send_sem=sent.at[stop],
            recv_sem=here.at[stop], device_id={"blk": peer(stop)}, device_id_type=MESH)

    others = [stop for stop in range(STOPS) if stop != LEAD]
    for stop in others:
        pl.semaphore_signal(
            barrier, inc=1, device_id={"blk": source(stop)}, device_id_type=MESH
        )
    pl.semaphore_wait(barrier, len(others))
    for stop in others:
        copy(stop).start()
    score_into(out, LEAD, queries, train)
    for stop in others:
        copy(stop).wait_recv()
        score_into(out, stop, held.at[stop], train)
    for stop in others:
        copy(stop).wait_send()


def grid_kernel(owners, queries, train, out, held, up_sent, down_sent, side_sent, twin_sent, here):
    lines = owners // 4
    me = lax.axis_index("blk")
    core = lax.rem(me, 2)
    side = lax.rem(me // 2, 2)
    line = me // 4
    twin = me + 1 - 2 * core
    across = me + 2 - 4 * side
    across_twin = across + 1 - 2 * core
    has_up, has_down = line + 1 < lines, line > 0

    def stop_of(device, origin):
        return lax.rem(device - origin + LEAD + owners, owners)

    def wants(device, origin):
        return stop_of(device, origin) < STOPS

    def copy(source, origin, sems, device):
        return pltpu.make_async_remote_copy(
            src_ref=source, dst_ref=held.at[origin], send_sem=sems.at[origin],
            recv_sem=here.at[origin], device_id={"blk": device}, device_id_type=MESH)

    barrier = pltpu.get_barrier_semaphore()

    def greet(device):
        pl.semaphore_signal(barrier, inc=1, device_id={"blk": device}, device_id_type=MESH)

    greet(twin)
    greet(across)
    pl.when(has_up)(lambda: greet(me + 4))
    pl.when(has_down)(lambda: greet(me - 4))
    pl.semaphore_wait(barrier, 2 + has_up.astype(jnp.int32) + has_down.astype(jnp.int32))

    pl.when(has_up)(lambda: copy(queries, me, up_sent, me + 4).start())
    pl.when(has_down)(lambda: copy(queries, me, down_sent, me - 4).start())
    copy(queries, me, side_sent, across).start()
    copy(queries, me, twin_sent, twin).start()
    held[me] = queries[...]

    def candidate(stage, index):
        way, column, plane = lax.rem(index, 2), lax.rem(index // 2, 2), index // 4
        distance = stage - column
        spot = line + distance * (2 * way - 1)
        near = lax.rem(side + column, 2)
        origin = (spot * 2 + near) * 2 + lax.rem(core + plane, 2)
        real = (spot >= 0) & (spot < lines) & (distance >= 0)
        real = real & ((distance > 0) | (way == 0))
        return way, column, plane, origin, real

    def passes(stage, index, act):
        way, column, _, origin, real = candidate(stage, index)
        straight = real & (column == 0)
        pl.when(straight & (way == 0) & has_up)(
            lambda: act(copy(held.at[origin], origin, up_sent, me + 4)))
        pl.when(straight & (way == 1) & has_down)(
            lambda: act(copy(held.at[origin], origin, down_sent, me - 4)))
        pl.when(straight & (wants(across, origin) | wants(across_twin, origin)))(
            lambda: act(copy(held.at[origin], origin, side_sent, across)))
        pl.when(real & ((column == 0) | wants(me, origin) | wants(twin, origin)) & wants(twin, origin))(
            lambda: act(copy(held.at[origin], origin, twin_sent, twin)))

    @pl.loop(0, lines + 1)
    def _(stage):
        @pl.when(stage > 0)
        def _():
            @pl.loop(0, 4)
            def _(index):
                _, column, _, origin, real = candidate(stage, index)
                comes = real & ((column == 0) | wants(me, origin) | wants(twin, origin))

                @pl.when(comes)
                def _():
                    copy(held.at[origin], origin, twin_sent, twin).wait_recv()

                passes(stage, index, lambda c: c.start())

        @pl.loop(0, 8)
        def _(index):
            _, _, plane, origin, real = candidate(stage, index)

            @pl.when(real & wants(me, origin))
            def _():
                @pl.when(plane == 1)
                def _():
                    copy(held.at[origin], origin, twin_sent, twin).wait_recv()

                score_into(out, stop_of(me, origin), held.at[origin], train)

    pl.when(has_up)(lambda: copy(queries, me, up_sent, me + 4).wait_send())
    pl.when(has_down)(lambda: copy(queries, me, down_sent, me - 4).wait_send())
    copy(queries, me, side_sent, across).wait_send()
    copy(queries, me, twin_sent, twin).wait_send()

    @pl.loop(1, lines + 1)
    def _(stage):
        @pl.loop(0, 4)
        def _(index):
            passes(stage, index, lambda c: c.wait_send())


def influence_of(queries, train):
    owners = lax.axis_size("blk")
    whole_grid = owners % 4 == 0 and owners < 2 * STOPS
    held = owners if whole_grid else STOPS
    kernel = grid_kernel if whole_grid else window_kernel
    return pl.pallas_call(
        functools.partial(kernel, owners),
        out_shape=jax.ShapeDtypeStruct((STOPS, DOC_DEV, train.shape[0]), BF16),
        in_specs=[VMEM_SPEC] * 2,
        out_specs=VMEM_SPEC,
        scratch_shapes=[pltpu.VMEM((held,) + queries.shape, BF16)]
        + [pltpu.SemaphoreType.DMA((held,))] * (5 if whole_grid else 2),
        compiler_params=pltpu.CompilerParams(collective_id=1, has_side_effects=True),
        name="influence",
    )(queries, train)


def local(query_inputs, query_grads, proj_in, proj_out, train_rows, token_owner, token_slot):
    recv_rows, recv_slot = dispatch(
        query_inputs, query_grads, proj_in, proj_out,
        token_owner, token_owner.reshape(1, -1), token_slot.reshape(1, -1),
    )
    return influence_of(make_queries(recv_rows, recv_slot), train_rows)


def solution(mesh):
    placed = (
        P(("groups", "blk"), None),
        P(("groups", "blk"), None),
        P(),
        P(),
        P(("groups", "blk"), None),
        P(("groups", "blk"), None),
        P(("groups", "blk")),
    )
    return jax.shard_map(
        local,
        mesh=mesh,
        in_specs=placed,
        out_specs=P(None, None, ("groups", "blk")),
        check_vma=False,
    )
```

```python
import functools

import jax
import jax.numpy as jnp
from jax import lax
from jax.experimental import pallas as pl
from jax.experimental.pallas import tpu as pltpu
from jax.sharding import PartitionSpec as P

DOC_DEV = 32
STOPS = 12
NEWTON_STEPS = 6
LEAD = 5
LANES = 128
DOC_GROUP = 8
GROUPS = DOC_DEV // DOC_GROUP
MESH = pl.DeviceIdType.MESH
VMEM_SPEC = pl.BlockSpec(memory_space=pltpu.VMEM)
F32 = jnp.float32
BF16 = jnp.bfloat16
CONTRACT_LAST = (((1,), (1,)), ((), ()))


def matmul(left, right):
    return jnp.dot(left, right, preferred_element_type=F32)


def halves(value):
    high = value.astype(BF16)
    return high, (value - high.astype(F32)).astype(BF16)


def split_matmul(left, right):
    left_high, left_low = left
    right_high, right_low = right
    joined = matmul(
        jnp.concatenate([left_high, left_low], axis=1),
        jnp.concatenate([right_high, right_high], axis=0),
    )
    return joined + matmul(left_high, right_low)


def dispatch_kernel(owners, capacity, x_in, x_grad, p_in, p_out, owner_row, slot_row,
                    recv_rows, recv_slot, low, send_rows, send_slot,
                    rows_sent, rows_here, slot_sent, slot_here):
    me = lax.axis_index("blk")
    barrier = pltpu.get_barrier_semaphore()

    @pl.loop(1, owners)
    def _(ahead):
        pl.semaphore_signal(
            barrier, inc=1, device_id={"blk": lax.rem(me + ahead, owners)}, device_id_type=MESH
        )

    count = x_in.shape[0]
    width = p_in.shape[0]
    for at, values, weights in ((0, x_grad, p_out), (width, x_in, p_in)):
        low[:, at:at + width] = lax.dot_general(
            values[...], weights[...], CONTRACT_LAST, preferred_element_type=F32
        ).astype(BF16)
    token = lax.broadcasted_iota(jnp.int32, (count, count), 0)
    other = lax.broadcasted_iota(jnp.int32, (count, count), 1)
    earlier = jnp.where(token < other, 1.0, 0.0).astype(BF16)
    owner_id = lax.broadcasted_iota(jnp.int32, (owners, count), 0)
    owner_hot = jnp.where(owner_id == owner_row[...], 1.0, 0.0)
    before = matmul(owner_hot.astype(BF16), earlier)
    rank = jnp.sum(before * owner_hot, axis=0, keepdims=True).astype(jnp.int32)
    position = owner_row[...] * capacity + rank
    place = lax.broadcasted_iota(jnp.int32, (owners * capacity, count), 0)
    placed = jnp.where(place == position, 1.0, 0.0).astype(BF16)
    send_rows[...] = matmul(placed, low[...]).astype(BF16).reshape(send_rows.shape)
    coded = jnp.where(owner_id == owner_row[...], slot_row[...] + 1, 0).astype(F32).astype(BF16)
    lane = lax.broadcasted_iota(jnp.int32, (LANES, count), 0)
    shift = lax.rem(me, LANES // capacity) * capacity
    spread = jnp.where(lane == rank + shift, 1.0, 0.0).astype(BF16)
    codes = lax.dot_general(coded, spread, CONTRACT_LAST, preferred_element_type=F32)
    codes = codes.astype(jnp.int32)
    for owner in range(owners):
        send_slot[owner] = codes[owner:owner + 1]
    pl.semaphore_wait(barrier, owners - 1)

    def copies(target, source, sem):
        to = {"blk": target}
        return (
            pltpu.make_async_remote_copy(
                src_ref=send_rows.at[target], dst_ref=recv_rows.at[source],
                send_sem=rows_sent.at[target], recv_sem=rows_here.at[sem],
                device_id=to, device_id_type=MESH),
            pltpu.make_async_remote_copy(
                src_ref=send_slot.at[target], dst_ref=recv_slot.at[source],
                send_sem=slot_sent.at[target], recv_sem=slot_here.at[sem],
                device_id=to, device_id_type=MESH),
        )

    @pl.loop(1, owners)
    def _(ahead):
        for copy in copies(lax.rem(me + ahead, owners), me, me):
            copy.start()

    recv_rows[me] = send_rows[me]
    recv_slot[me] = send_slot[me]

    @pl.loop(1, owners)
    def _(ahead):
        source = lax.rem(me + ahead, owners)
        for copy in copies(source, source, source):
            copy.wait_recv()

    @pl.loop(1, owners)
    def _(ahead):
        for copy in copies(lax.rem(me + ahead, owners), me, me):
            copy.wait_send()


def dispatch(x_in, x_grad, p_in, p_out, owner_row, slot_row):
    owners = lax.axis_size("blk")
    count, width = x_in.shape[0], p_in.shape[0]
    capacity = 4 * count // owners
    rows = (owners, capacity, 2 * width)
    slots = (owners, 1, LANES)
    return pl.pallas_call(
        functools.partial(dispatch_kernel, owners, capacity),
        out_shape=(jax.ShapeDtypeStruct(rows, BF16), jax.ShapeDtypeStruct(slots, jnp.int32)),
        in_specs=[VMEM_SPEC] * 6,
        out_specs=(VMEM_SPEC, VMEM_SPEC),
        scratch_shapes=[
            pltpu.VMEM((count, 2 * width), BF16),
            pltpu.VMEM(rows, BF16),
            pltpu.VMEM(slots, jnp.int32),
        ] + [pltpu.SemaphoreType.DMA((owners,))] * 4,
        compiler_params=pltpu.CompilerParams(collective_id=0, has_side_effects=True),
        name="dispatch",
    )(x_in, x_grad, p_in, p_out, owner_row, slot_row)


def prepare(recv_rows, recv_slot, turned, codes):
    owners, capacity, full = recv_rows.shape
    total = owners * capacity
    group = LANES // capacity
    rows = recv_rows[...].reshape(total, full)
    for part in range(total // LANES):
        span = slice(part * LANES, (part + 1) * LANES)
        turned[:, span] = rows[span].T
        code = recv_slot[part * group]
        for source in range(part * group + 1, (part + 1) * group):
            code = code + recv_slot[source]
        codes[:, span] = code


def query_group(step, recv_rows, turned, codes, flat, out):
    owners, capacity, full = recv_rows.shape
    width = full // 2
    row = lax.broadcasted_iota(jnp.int32, (full, full), 0)
    col = lax.broadcasted_iota(jnp.int32, (full, full), 1)
    upper_row = row < width
    diagonal = upper_row == (col < width)
    corner = upper_row & (col >= width)
    identity_mat = jnp.where(row == col, 1.0, 0.0)
    upper = lax.broadcasted_iota(jnp.int32, (full, 1), 0) < width
    docs = range(DOC_GROUP)
    code = codes[...]
    counts, masked = [], []
    for doc in docs:
        hot = jnp.where(code == step * DOC_GROUP + doc + 1, 1.0, 0.0)
        counts.append(jnp.sum(hot, axis=1, keepdims=True))
        masked.append(turned[...] * hot.astype(BF16))
    rows = recv_rows[...].reshape(owners * capacity, full)
    grams = matmul(jnp.concatenate(masked, axis=0), rows)
    grams = [grams[doc * full:(doc + 1) * full] for doc in docs]
    powers, approx = [], []
    for doc in docs:
        damped = jnp.where(diagonal, grams[doc] / (counts[doc] + 1.0), 0.0) + identity_mat
        sums = jnp.sum(jnp.abs(damped), axis=1, keepdims=True)
        bound = jnp.where(
            upper,
            jnp.max(sums[:width], axis=0, keepdims=True),
            jnp.max(sums[width:], axis=0, keepdims=True),
        )
        scale = 1.0 / bound
        residual = identity_mat - damped * scale
        approx.append((identity_mat + residual) * scale)
        parts = halves(residual)
        powers.append(split_matmul(parts, parts))
    for level in range(NEWTON_STEPS - 2):
        for doc in docs:
            power = halves(powers[doc])
            inverse = halves(approx[doc])
            both = tuple(jnp.concatenate([p, x], axis=1) for p, x in zip(power, inverse))
            product = split_matmul(power, both)
            powers[doc] = product[:, :full]
            approx[doc] = approx[doc] + product[:, full:]
    for doc in docs:
        inverse = approx[doc] + split_matmul(halves(powers[doc]), halves(approx[doc]))
        mixed = jnp.where(corner, grams[doc], 0.0)
        tilted = split_matmul(halves(inverse[:width]), halves(mixed))
        right = inverse[width:]
        right = right + pltpu.roll(right, width, 1)
        right = jnp.concatenate([jnp.zeros_like(right), right], axis=0)
        flat[doc * width:(doc + 1) * width, :] = split_matmul(halves(tilted), halves(right))

    left = lax.broadcasted_iota(jnp.int32, (DOC_GROUP, full), 1) < width
    for pair in range(width // 2):
        even = flat[pl.ds(2 * pair, DOC_GROUP, stride=width), :]
        odd = flat[pl.ds(2 * pair + 1, DOC_GROUP, stride=width), :]
        out[:, pair * full:(pair + 1) * full] = jnp.where(left, even, odd).astype(BF16)


def query_scratch(recv_rows):
    owners, capacity, full = recv_rows.shape
    total = owners * capacity
    return [
        pltpu.VMEM((full, total), BF16),
        pltpu.VMEM((1, total), jnp.int32),
        pltpu.VMEM((DOC_GROUP * (full // 2), full), F32),
    ]


def queries_kernel(recv_rows, recv_slot, out, turned, codes, flat):
    prepare(recv_rows, recv_slot, turned, codes)

    @pl.loop(0, GROUPS)
    def _(step):
        query_group(step, recv_rows, turned, codes, flat, out.at[step])


def make_queries(recv_rows, recv_slot):
    width = recv_rows.shape[2] // 2
    return pl.pallas_call(
        queries_kernel,
        out_shape=jax.ShapeDtypeStruct((GROUPS, DOC_GROUP, width * width), BF16),
        in_specs=[VMEM_SPEC] * 2,
        out_specs=VMEM_SPEC,
        scratch_shapes=query_scratch(recv_rows),
        name="queries",
    )(recv_rows, recv_slot).reshape(DOC_DEV, width * width)


def score_into(out, index, block, train):
    out[index] = lax.dot_general(
        block[...], train[...], CONTRACT_LAST, preferred_element_type=F32
    ).astype(BF16)


def window_kernel(owners, queries, train, out, held, sent, here):
    me = lax.axis_index("blk")
    barrier = pltpu.get_barrier_semaphore()

    def peer(stop):
        return lax.rem(me + stop - LEAD + owners, owners)

    def source(stop):
        return lax.rem(me - stop + LEAD + owners, owners)

    def copy(stop):
        return pltpu.make_async_remote_copy(
            src_ref=queries, dst_ref=held.at[stop], send_sem=sent.at[stop],
            recv_sem=here.at[stop], device_id={"blk": peer(stop)}, device_id_type=MESH)

    others = [stop for stop in range(STOPS) if stop != LEAD]
    for stop in others:
        pl.semaphore_signal(
            barrier, inc=1, device_id={"blk": source(stop)}, device_id_type=MESH
        )
    pl.semaphore_wait(barrier, len(others))
    for stop in others:
        copy(stop).start()
    score_into(out, LEAD, queries, train)
    for stop in others:
        copy(stop).wait_recv()
        score_into(out, stop, held.at[stop], train)
    for stop in others:
        copy(stop).wait_send()


def grid_kernel(owners, recv_rows, recv_slot, train, out, turned, codes, flat, held,
                up_sent, down_sent, side_sent, twin_sent, here):
    lines = owners // 4
    me = lax.axis_index("blk")
    core = lax.rem(me, 2)
    side = lax.rem(me // 2, 2)
    line = me // 4
    twin = me + 1 - 2 * core
    across = me + 2 - 4 * side
    across_twin = across + 1 - 2 * core
    above, below = me + 4, me - 4
    has_up, has_down = line + 1 < lines, line > 0

    def stop_of(device, origin):
        return lax.rem(device - origin + LEAD + owners, owners)

    def wants(device, origin):
        return stop_of(device, origin) < STOPS

    def copy(group, origin, sems, device):
        mine, theirs = stop_of(me, origin), stop_of(device, origin)
        return pltpu.make_async_remote_copy(
            src_ref=held.at[group, mine], dst_ref=held.at[group, theirs],
            send_sem=sems.at[group, mine], recv_sem=here.at[group, theirs],
            device_id={"blk": device}, device_id_type=MESH)

    def arrive(group, origin):
        mine = stop_of(me, origin)
        pltpu.make_async_remote_copy(
            src_ref=held.at[group, mine], dst_ref=held.at[group, mine],
            send_sem=twin_sent.at[group, mine], recv_sem=here.at[group, mine],
            device_id={"blk": twin}, device_id_type=MESH).wait_recv()

    barrier = pltpu.get_barrier_semaphore()

    def greet(device):
        pl.semaphore_signal(barrier, inc=1, device_id={"blk": device}, device_id_type=MESH)

    greet(twin)
    greet(across)
    pl.when(has_up)(lambda: greet(above))
    pl.when(has_down)(lambda: greet(below))
    prepare(recv_rows, recv_slot, turned, codes)

    def candidate(stage, index):
        way, column, plane = lax.rem(index, 2), lax.rem(index // 2, 2), index // 4
        distance = stage - column
        spot = line + distance * (2 * way - 1)
        near = lax.rem(side + column, 2)
        origin = (spot * 2 + near) * 2 + lax.rem(core + plane, 2)
        real = (spot >= 0) & (spot < lines) & (distance >= 0)
        real = real & ((distance > 0) | (way == 0))
        return way, column, origin, real

    def comes(column, origin, real):
        return real & ((column == 0) | wants(me, origin) | wants(twin, origin))

    def passes(group, stage, index, act):
        way, column, origin, real = candidate(stage, index)
        straight = real & (column == 0)
        pl.when(straight & ((way == 0) | (stage == 0)) & has_up)(
            lambda: act(copy(group, origin, up_sent, above)))
        pl.when(straight & ((way == 1) | (stage == 0)) & has_down)(
            lambda: act(copy(group, origin, down_sent, below)))
        pl.when(straight & (wants(across, origin) | wants(across_twin, origin)))(
            lambda: act(copy(group, origin, side_sent, across)))
        pl.when(comes(column, origin, real) & wants(twin, origin))(
            lambda: act(copy(group, origin, twin_sent, twin)))

    @pl.loop(0, GROUPS + lines)
    def _(step):
        @pl.when(step < GROUPS)
        def _():
            query_group(step, recv_rows, turned, codes, flat, held.at[step, LEAD])

            @pl.when(step == 0)
            def _():
                pl.semaphore_wait(barrier, 2 + has_up.astype(jnp.int32) + has_down.astype(jnp.int32))

            passes(step, 0, 0, lambda c: c.start())

        @pl.loop(0, lines)
        def _(back):
            stage = lines - back
            group = step - stage

            @pl.when((group >= 0) & (group < GROUPS))
            def _():
                @pl.loop(0, 4)
                def _(index):
                    _, column, origin, real = candidate(stage, index)

                    @pl.when(comes(column, origin, real))
                    def _():
                        arrive(group, origin)

                    passes(group, stage, index, lambda c: c.start())

        @pl.when(step >= lines)
        def _():
            group = step - lines

            @pl.loop(0, lines + 1)
            def _(stage):
                @pl.loop(4, 8)
                def _(index):
                    _, _, origin, real = candidate(stage, index)

                    @pl.when(real & wants(me, origin))
                    def _():
                        arrive(group, origin)

            block = held[group, :STOPS].reshape(STOPS * DOC_GROUP, train.shape[1])
            tile = lax.dot_general(block, train[...], CONTRACT_LAST, preferred_element_type=F32)
            out[group] = tile.astype(BF16).reshape(STOPS, DOC_GROUP, train.shape[0])

    @pl.loop(0, GROUPS)
    def _(group):
        passes(group, 0, 0, lambda c: c.wait_send())

        @pl.loop(1, lines + 1)
        def _(stage):
            @pl.loop(0, 4)
            def _(index):
                passes(group, stage, index, lambda c: c.wait_send())


def influence_of(recv_rows, recv_slot, train):
    owners = lax.axis_size("blk")
    params = pltpu.CompilerParams(collective_id=1, has_side_effects=True)
    if owners % 4 == 0 and owners < 2 * STOPS:
        tiles = pl.pallas_call(
            functools.partial(grid_kernel, owners),
            out_shape=jax.ShapeDtypeStruct((GROUPS, STOPS, DOC_GROUP, train.shape[0]), BF16),
            in_specs=[VMEM_SPEC] * 3,
            out_specs=VMEM_SPEC,
            scratch_shapes=query_scratch(recv_rows)
            + [pltpu.VMEM((GROUPS, owners, DOC_GROUP, train.shape[1]), BF16)]
            + [pltpu.SemaphoreType.DMA((GROUPS, owners))] * 5,
            compiler_params=params,
            name="influence",
        )(recv_rows, recv_slot, train)
        return tiles.transpose(1, 0, 2, 3).reshape(STOPS, DOC_DEV, train.shape[0])
    queries = make_queries(recv_rows, recv_slot)
    return pl.pallas_call(
        functools.partial(window_kernel, owners),
        out_shape=jax.ShapeDtypeStruct((STOPS, DOC_DEV, train.shape[0]), BF16),
        in_specs=[VMEM_SPEC] * 2,
        out_specs=VMEM_SPEC,
        scratch_shapes=[pltpu.VMEM((STOPS,) + queries.shape, BF16)]
        + [pltpu.SemaphoreType.DMA((STOPS,))] * 2,
        compiler_params=params,
        name="influence",
    )(queries, train)


def local(query_inputs, query_grads, proj_in, proj_out, train_rows, token_owner, token_slot):
    recv_rows, recv_slot = dispatch(
        query_inputs, query_grads, proj_in.T, proj_out.T,
        token_owner.reshape(1, -1), token_slot.reshape(1, -1),
    )
    return influence_of(recv_rows, recv_slot, train_rows)


def solution(mesh):
    placed = (
        P(("groups", "blk"), None),
        P(("groups", "blk"), None),
        P(),
        P(),
        P(("groups", "blk"), None),
        P(("groups", "blk"), None),
        P(("groups", "blk")),
    )
    return jax.shard_map(
        local,
        mesh=mesh,
        in_specs=placed,
        out_specs=P(None, None, ("groups", "blk")),
        check_vma=False,
    )
```

```python
import functools

import jax
import jax.numpy as jnp
from jax import lax
from jax.experimental import pallas as pl
from jax.experimental.pallas import tpu as pltpu
from jax.sharding import PartitionSpec as P

DOC_DEV = 32
STOPS = 12
NEWTON_STEPS = 6
LEAD = 5
LANES = 128
DOC_GROUP = 8
GROUPS = DOC_DEV // DOC_GROUP
MESH = pl.DeviceIdType.MESH
VMEM_SPEC = pl.BlockSpec(memory_space=pltpu.VMEM)
F32 = jnp.float32
BF16 = jnp.bfloat16
CONTRACT_LAST = (((1,), (1,)), ((), ()))


def matmul(left, right):
    return jnp.dot(left, right, preferred_element_type=F32)


def halves(value):
    high = value.astype(BF16)
    return high, (value - high.astype(F32)).astype(BF16)


def left_parts(value, right_half):
    width = value.shape[1] // 2
    high = value.astype(BF16).astype(F32)
    low = value - high
    if right_half:
        high = pltpu.roll(high, width, 1)
    else:
        low = pltpu.roll(low, width, 1)
    is_left = lax.broadcasted_iota(jnp.int32, value.shape, 1) < width
    parts = jnp.where(is_left, high, low).astype(BF16)
    return jnp.concatenate([parts, parts], axis=1)


def pair_product(lefts, rights, right_half):
    high, low = zip(*[halves(value) for value in rights])
    high, low = jnp.concatenate(high, axis=1), jnp.concatenate(low, axis=1)
    product = matmul(
        jnp.concatenate([left_parts(value, right_half) for value in lefts], axis=0),
        jnp.concatenate([high, high, low, low], axis=0),
    )
    rows, cols = lefts[0].shape
    return product[:rows, :cols], product[rows:, cols:]


def dispatch_kernel(owners, capacity, x_in, x_grad, p_in, p_out, owner_row, slot_row,
                    recv_rows, recv_slot, low, send_rows, send_slot,
                    rows_sent, rows_here, slot_sent, slot_here):
    me = lax.axis_index("blk")
    barrier = pltpu.get_barrier_semaphore()

    @pl.loop(1, owners)
    def _(ahead):
        pl.semaphore_signal(
            barrier, inc=1, device_id={"blk": lax.rem(me + ahead, owners)}, device_id_type=MESH
        )

    count = x_in.shape[0]
    width = p_in.shape[0]
    for at, values, weights in ((0, x_grad, p_out), (width, x_in, p_in)):
        low[:, at:at + width] = lax.dot_general(
            values[...], weights[...], CONTRACT_LAST, preferred_element_type=F32
        ).astype(BF16)
    token = lax.broadcasted_iota(jnp.int32, (count, count), 0)
    other = lax.broadcasted_iota(jnp.int32, (count, count), 1)
    earlier = jnp.where(token < other, 1.0, 0.0).astype(BF16)
    owner_id = lax.broadcasted_iota(jnp.int32, (owners, count), 0)
    owner_hot = jnp.where(owner_id == owner_row[...], 1.0, 0.0)
    before = matmul(owner_hot.astype(BF16), earlier)
    rank = jnp.sum(before * owner_hot, axis=0, keepdims=True).astype(jnp.int32)
    position = owner_row[...] * capacity + rank
    place = lax.broadcasted_iota(jnp.int32, (owners * capacity, count), 0)
    placed = jnp.where(place == position, 1.0, 0.0).astype(BF16)
    send_rows[...] = matmul(placed, low[...]).astype(BF16).reshape(send_rows.shape)
    coded = jnp.where(owner_id == owner_row[...], slot_row[...] + 1, 0).astype(F32).astype(BF16)
    lane = lax.broadcasted_iota(jnp.int32, (LANES, count), 0)
    shift = lax.rem(me, LANES // capacity) * capacity
    spread = jnp.where(lane == rank + shift, 1.0, 0.0).astype(BF16)
    codes = lax.dot_general(coded, spread, CONTRACT_LAST, preferred_element_type=F32)
    codes = codes.astype(jnp.int32)
    for owner in range(owners):
        send_slot[owner] = codes[owner:owner + 1]
    pl.semaphore_wait(barrier, owners - 1)

    def copies(target, source, sem):
        to = {"blk": target}
        return (
            pltpu.make_async_remote_copy(
                src_ref=send_rows.at[target], dst_ref=recv_rows.at[source],
                send_sem=rows_sent.at[target], recv_sem=rows_here.at[sem],
                device_id=to, device_id_type=MESH),
            pltpu.make_async_remote_copy(
                src_ref=send_slot.at[target], dst_ref=recv_slot.at[source],
                send_sem=slot_sent.at[target], recv_sem=slot_here.at[sem],
                device_id=to, device_id_type=MESH),
        )

    @pl.loop(1, owners)
    def _(ahead):
        for copy in copies(lax.rem(me + ahead, owners), me, me):
            copy.start()

    recv_rows[me] = send_rows[me]
    recv_slot[me] = send_slot[me]

    @pl.loop(1, owners)
    def _(ahead):
        source = lax.rem(me + ahead, owners)
        for copy in copies(source, source, source):
            copy.wait_recv()

    @pl.loop(1, owners)
    def _(ahead):
        for copy in copies(lax.rem(me + ahead, owners), me, me):
            copy.wait_send()


def dispatch(x_in, x_grad, p_in, p_out, owner_row, slot_row):
    owners = lax.axis_size("blk")
    count, width = x_in.shape[0], p_in.shape[0]
    capacity = 4 * count // owners
    rows = (owners, capacity, 2 * width)
    slots = (owners, 1, LANES)
    return pl.pallas_call(
        functools.partial(dispatch_kernel, owners, capacity),
        out_shape=(jax.ShapeDtypeStruct(rows, BF16), jax.ShapeDtypeStruct(slots, jnp.int32)),
        in_specs=[VMEM_SPEC] * 6,
        out_specs=(VMEM_SPEC, VMEM_SPEC),
        scratch_shapes=[
            pltpu.VMEM((count, 2 * width), BF16),
            pltpu.VMEM(rows, BF16),
            pltpu.VMEM(slots, jnp.int32),
        ] + [pltpu.SemaphoreType.DMA((owners,))] * 4,
        compiler_params=pltpu.CompilerParams(collective_id=0, has_side_effects=True),
        name="dispatch",
    )(x_in, x_grad, p_in, p_out, owner_row, slot_row)


def prepare(recv_rows, recv_slot, turned, codes):
    owners, capacity, full = recv_rows.shape
    total = owners * capacity
    group = LANES // capacity
    rows = recv_rows[...].reshape(total, full)
    for part in range(total // LANES):
        span = slice(part * LANES, (part + 1) * LANES)
        turned[:, span] = rows[span].T
        code = recv_slot[part * group]
        for source in range(part * group + 1, (part + 1) * group):
            code = code + recv_slot[source]
        codes[:, span] = code


def query_group(step, recv_rows, turned, codes, flat, out):
    owners, capacity, full = recv_rows.shape
    width = full // 2
    row = lax.broadcasted_iota(jnp.int32, (width, full), 0)
    col = lax.broadcasted_iota(jnp.int32, (width, full), 1)
    left = col < width
    left_eye = jnp.where(row == col, 1.0, 0.0)
    right_eye = jnp.where(row + width == col, 1.0, 0.0)
    docs = range(DOC_GROUP)
    code = codes[...]
    counts, masked = [], []
    for doc in docs:
        hot = jnp.where(code == step * DOC_GROUP + doc + 1, 1.0, 0.0)
        counts.append(jnp.sum(hot, axis=1, keepdims=True))
        masked.append(turned[...] * hot.astype(BF16))
    rows = recv_rows[...].reshape(owners * capacity, full)
    grams = matmul(jnp.concatenate(masked, axis=0), rows)
    crossed, states = [], []
    for doc in docs:
        top = grams[doc * full:doc * full + width]
        bottom = grams[doc * full + width:(doc + 1) * full]
        crossed.append(top)
        pair = []
        for outer in (top, pltpu.roll(bottom, width, 1)):
            damped = jnp.where(left, outer / (counts[doc] + 1.0), 0.0) + left_eye
            sums = jnp.sum(jnp.abs(damped), axis=1, keepdims=True)
            scale = 1.0 / jnp.max(sums, axis=0, keepdims=True)
            pair.append(left_eye - damped * scale + right_eye * scale)
        states.append(pair)
    for level in range(NEWTON_STEPS):
        for doc in docs:
            products = pair_product(states[doc], states[doc], False)
            states[doc] = [
                product + jnp.where(left, 0.0, state)
                for product, state in zip(products, states[doc])
            ]
    for doc in range(0, DOC_GROUP, 2):
        pair = (doc, doc + 1)
        tilted = pair_product(
            [states[d][0] for d in pair], [crossed[d] for d in pair], True)
        tilted = pair_product(tilted, [states[d][1] for d in pair], True)
        for d, value in zip(pair, tilted):
            flat[d * width:(d + 1) * width, :] = value

    near = lax.broadcasted_iota(jnp.int32, (DOC_GROUP, full), 1) < width
    for pair in range(width // 2):
        even = flat[pl.ds(2 * pair, DOC_GROUP, stride=width), :]
        odd = flat[pl.ds(2 * pair + 1, DOC_GROUP, stride=width), :]
        both = jnp.where(near, pltpu.roll(even, width, 1), odd)
        out[:, pair * full:(pair + 1) * full] = both.astype(BF16)


def query_scratch(recv_rows):
    owners, capacity, full = recv_rows.shape
    total = owners * capacity
    return [
        pltpu.VMEM((full, total), BF16),
        pltpu.VMEM((1, total), jnp.int32),
        pltpu.VMEM((DOC_GROUP * (full // 2), full), F32),
    ]


def queries_kernel(recv_rows, recv_slot, out, turned, codes, flat):
    prepare(recv_rows, recv_slot, turned, codes)

    @pl.loop(0, GROUPS)
    def _(step):
        query_group(step, recv_rows, turned, codes, flat, out.at[step])


def make_queries(recv_rows, recv_slot):
    width = recv_rows.shape[2] // 2
    return pl.pallas_call(
        queries_kernel,
        out_shape=jax.ShapeDtypeStruct((GROUPS, DOC_GROUP, width * width), BF16),
        in_specs=[VMEM_SPEC] * 2,
        out_specs=VMEM_SPEC,
        scratch_shapes=query_scratch(recv_rows),
        name="queries",
    )(recv_rows, recv_slot).reshape(DOC_DEV, width * width)


def score_into(out, index, block, train):
    out[index] = lax.dot_general(
        block[...], train[...], CONTRACT_LAST, preferred_element_type=F32
    ).astype(BF16)


def window_kernel(owners, queries, train, out, held, sent, here):
    me = lax.axis_index("blk")
    barrier = pltpu.get_barrier_semaphore()

    def peer(stop):
        return lax.rem(me + stop - LEAD + owners, owners)

    def source(stop):
        return lax.rem(me - stop + LEAD + owners, owners)

    def copy(stop):
        return pltpu.make_async_remote_copy(
            src_ref=queries, dst_ref=held.at[stop], send_sem=sent.at[stop],
            recv_sem=here.at[stop], device_id={"blk": peer(stop)}, device_id_type=MESH)

    others = [stop for stop in range(STOPS) if stop != LEAD]
    for stop in others:
        pl.semaphore_signal(
            barrier, inc=1, device_id={"blk": source(stop)}, device_id_type=MESH
        )
    pl.semaphore_wait(barrier, len(others))
    for stop in others:
        copy(stop).start()
    score_into(out, LEAD, queries, train)
    for stop in others:
        copy(stop).wait_recv()
        score_into(out, stop, held.at[stop], train)
    for stop in others:
        copy(stop).wait_send()


def grid_kernel(owners, recv_rows, recv_slot, train, out, turned, codes, flat, held,
                up_sent, down_sent, side_sent, twin_sent, here):
    lines = owners // 4
    me = lax.axis_index("blk")
    core = lax.rem(me, 2)
    side = lax.rem(me // 2, 2)
    line = me // 4
    twin = me + 1 - 2 * core
    across = me + 2 - 4 * side
    to_twin, to_across = 1 - 2 * core, 2 - 4 * side
    above, below = me + 4, me - 4
    has_up, has_down = line + 1 < lines, line > 0

    barrier = pltpu.get_barrier_semaphore()

    def greet(device):
        pl.semaphore_signal(barrier, inc=1, device_id={"blk": device}, device_id_type=MESH)

    greet(twin)
    greet(across)
    pl.when(has_up)(lambda: greet(above))
    pl.when(has_down)(lambda: greet(below))
    prepare(recv_rows, recv_slot, turned, codes)

    def wrapped(stop):
        return stop % owners if isinstance(stop, int) else lax.rem(stop + 3 * owners, owners)

    def wanted(stop):
        return wrapped(stop) < STOPS

    def either(first, second):
        return True if first is True or second is True else first | second

    def both(first, second):
        if first is True or second is True:
            return second if first is True else first
        return first & second

    def when(wish, act):
        if wish is True:
            act()
        elif wish is not False:
            pl.when(wish)(act)

    def reached(distance, way):
        if distance == 0:
            return True
        return line >= distance if way == 0 else line < lines - distance

    def place(stage, way, column):
        distance = stage - column
        if distance < 0 or (distance == 0 and way == 1):
            return None
        stop = LEAD - 4 * distance * (2 * way - 1)
        if column:
            stop = stop - to_across
        real = reached(distance, way)
        hands = []
        if column == 0:
            if way == 0:
                hands.append((both(real, has_up), 0, above, stop + 4))
            if way == 1 or distance == 0:
                hands.append((both(real, has_down), 1, below, stop - 4))
            sideways = either(wanted(stop + to_across), wanted(stop + to_across + to_twin))
            if distance == 0:
                sideways = True
            hands.append((both(real, sideways), 2, across, stop + to_across))
        else:
            real = both(real, either(wanted(stop), wanted(stop + to_twin)))
        hands.append((both(real, wanted(stop + to_twin)), 3, twin, stop + to_twin))
        twin_stop = stop - to_twin
        from_twin = both(reached(distance, way), wanted(twin_stop))
        hands = [(wish, sem, device, wrapped(theirs)) for wish, sem, device, theirs in hands]
        return wrapped(stop), real, hands, wrapped(twin_stop), from_twin

    sems = (up_sent, down_sent, side_sent, twin_sent)
    stages = []
    for stage in range(lines + 1):
        found = [place(stage, way, column) for column in range(2) for way in range(2)]
        stages.append([item for item in found if item is not None])

    def copy(group, mine, sem, device, theirs):
        return pltpu.make_async_remote_copy(
            src_ref=held.at[group, mine], dst_ref=held.at[group, theirs],
            send_sem=sems[sem].at[group, mine], recv_sem=here.at[group, theirs],
            device_id={"blk": device}, device_id_type=MESH)

    def arrive(group, mine):
        copy(group, mine, 3, twin, mine).wait_recv()

    def hand_on(group, item):
        for wish, sem, device, theirs in item[2]:
            when(wish, lambda: copy(group, item[0], sem, device, theirs).start())

    @pl.loop(0, GROUPS + lines)
    def _(step):
        @pl.when(step < GROUPS)
        def _():
            query_group(step, recv_rows, turned, codes, flat, held.at[step, LEAD])

            @pl.when(step == 0)
            def _():
                pl.semaphore_wait(barrier, 2 + has_up.astype(jnp.int32) + has_down.astype(jnp.int32))

            hand_on(step, stages[0][0])

        for stage in range(lines, 0, -1):
            group = step - stage

            @pl.when((group >= 0) & (group < GROUPS))
            def _():
                for item in stages[stage]:
                    when(item[1], lambda: arrive(group, item[0]))
                    hand_on(group, item)

        @pl.when(step >= lines)
        def _():
            group = step - lines
            for items in stages:
                for _, _, _, twin_stop, from_twin in items:
                    when(from_twin, lambda: arrive(group, twin_stop))
            block = held[group, :STOPS].reshape(STOPS * DOC_GROUP, train.shape[1])
            tile = lax.dot_general(block, train[...], CONTRACT_LAST, preferred_element_type=F32)
            out[group] = tile.astype(BF16).reshape(STOPS, DOC_GROUP, train.shape[0])

    @pl.loop(0, GROUPS)
    def _(group):
        for items in stages:
            for item in items:
                for wish, sem, device, theirs in item[2]:
                    when(wish, lambda: copy(group, item[0], sem, device, theirs).wait_send())


def influence_of(recv_rows, recv_slot, train):
    owners = lax.axis_size("blk")
    params = pltpu.CompilerParams(collective_id=1, has_side_effects=True)
    if owners % 4 == 0 and owners < 2 * STOPS:
        tiles = pl.pallas_call(
            functools.partial(grid_kernel, owners),
            out_shape=jax.ShapeDtypeStruct((GROUPS, STOPS, DOC_GROUP, train.shape[0]), BF16),
            in_specs=[VMEM_SPEC] * 3,
            out_specs=VMEM_SPEC,
            scratch_shapes=query_scratch(recv_rows)
            + [pltpu.VMEM((GROUPS, owners, DOC_GROUP, train.shape[1]), BF16)]
            + [pltpu.SemaphoreType.DMA((GROUPS, owners))] * 5,
            compiler_params=params,
            name="influence",
        )(recv_rows, recv_slot, train)
        return tiles.transpose(1, 0, 2, 3).reshape(STOPS, DOC_DEV, train.shape[0])
    queries = make_queries(recv_rows, recv_slot)
    return pl.pallas_call(
        functools.partial(window_kernel, owners),
        out_shape=jax.ShapeDtypeStruct((STOPS, DOC_DEV, train.shape[0]), BF16),
        in_specs=[VMEM_SPEC] * 2,
        out_specs=VMEM_SPEC,
        scratch_shapes=[pltpu.VMEM((STOPS,) + queries.shape, BF16)]
        + [pltpu.SemaphoreType.DMA((STOPS,))] * 2,
        compiler_params=params,
        name="influence",
    )(queries, train)


def local(query_inputs, query_grads, proj_in, proj_out, train_rows, token_owner, token_slot):
    recv_rows, recv_slot = dispatch(
        query_inputs, query_grads, proj_in.T, proj_out.T,
        token_owner.reshape(1, -1), token_slot.reshape(1, -1),
    )
    return influence_of(recv_rows, recv_slot, train_rows)


def solution(mesh):
    placed = (
        P(("groups", "blk"), None),
        P(("groups", "blk"), None),
        P(),
        P(),
        P(("groups", "blk"), None),
        P(("groups", "blk"), None),
        P(("groups", "blk")),
    )
    return jax.shard_map(
        local,
        mesh=mesh,
        in_specs=placed,
        out_specs=P(None, None, ("groups", "blk")),
        check_vma=False,
    )
```

```python
import functools

import jax
import jax.numpy as jnp
from jax import lax
from jax.experimental import pallas as pl
from jax.experimental.pallas import tpu as pltpu
from jax.sharding import PartitionSpec as P

DOC_DEV = 32
STOPS = 12
NEWTON_STEPS = 6
LEAD = 5
LANES = 128
DOC_GROUP = 8
GROUPS = DOC_DEV // DOC_GROUP
MESH = pl.DeviceIdType.MESH
VMEM_SPEC = pl.BlockSpec(memory_space=pltpu.VMEM)
F32 = jnp.float32
BF16 = jnp.bfloat16
CONTRACT_LAST = (((1,), (1,)), ((), ()))


def matmul(left, right):
    return jnp.dot(left, right, preferred_element_type=F32)


def halves(value):
    high = value.astype(BF16)
    return high, (value - high.astype(F32)).astype(BF16)


def left_parts(value, right_half):
    width = value.shape[1] // 2
    high = value.astype(BF16).astype(F32)
    low = value - high
    if right_half:
        high = pltpu.roll(high, width, 1)
    else:
        low = pltpu.roll(low, width, 1)
    is_left = lax.broadcasted_iota(jnp.int32, value.shape, 1) < width
    parts = jnp.where(is_left, high, low).astype(BF16)
    return jnp.concatenate([parts, parts], axis=1)


def pair_product(lefts, rights, right_half):
    high, low = zip(*[halves(value) for value in rights])
    high, low = jnp.concatenate(high, axis=1), jnp.concatenate(low, axis=1)
    product = matmul(
        jnp.concatenate([left_parts(value, right_half) for value in lefts], axis=0),
        jnp.concatenate([high, high, low, low], axis=0),
    )
    rows, cols = lefts[0].shape
    return product[:rows, :cols], product[rows:, cols:]


def dispatch_kernel(owners, capacity, x_in, x_grad, p_in, p_out, owner_row, slot_row,
                    recv_rows, recv_slot, low, send_rows, send_slot,
                    rows_sent, rows_here, slot_sent, slot_here):
    me = lax.axis_index("blk")
    barrier = pltpu.get_barrier_semaphore()

    @pl.loop(1, owners)
    def _(ahead):
        pl.semaphore_signal(
            barrier, inc=1, device_id={"blk": lax.rem(me + ahead, owners)}, device_id_type=MESH
        )

    count = x_in.shape[0]
    width = p_in.shape[0]
    for at, values, weights in ((0, x_grad, p_out), (width, x_in, p_in)):
        low[:, at:at + width] = lax.dot_general(
            values[...], weights[...], CONTRACT_LAST, preferred_element_type=F32
        ).astype(BF16)
    token = lax.broadcasted_iota(jnp.int32, (count, count), 0)
    other = lax.broadcasted_iota(jnp.int32, (count, count), 1)
    earlier = jnp.where(token < other, 1.0, 0.0).astype(BF16)
    owner_id = lax.broadcasted_iota(jnp.int32, (owners, count), 0)
    owner_hot = jnp.where(owner_id == owner_row[...], 1.0, 0.0)
    before = matmul(owner_hot.astype(BF16), earlier)
    rank = jnp.sum(before * owner_hot, axis=0, keepdims=True).astype(jnp.int32)
    position = owner_row[...] * capacity + rank
    place = lax.broadcasted_iota(jnp.int32, (owners * capacity, count), 0)
    placed = jnp.where(place == position, 1.0, 0.0).astype(BF16)
    send_rows[...] = matmul(placed, low[...]).astype(BF16).reshape(send_rows.shape)
    coded = jnp.where(owner_id == owner_row[...], slot_row[...] + 1, 0).astype(F32).astype(BF16)
    lane = lax.broadcasted_iota(jnp.int32, (LANES, count), 0)
    shift = lax.rem(me, LANES // capacity) * capacity
    spread = jnp.where(lane == rank + shift, 1.0, 0.0).astype(BF16)
    codes = lax.dot_general(coded, spread, CONTRACT_LAST, preferred_element_type=F32)
    codes = codes.astype(jnp.int32)
    for owner in range(owners):
        send_slot[owner] = codes[owner:owner + 1]
    pl.semaphore_wait(barrier, owners - 1)

    def copies(target, source, sem):
        to = {"blk": target}
        return (
            pltpu.make_async_remote_copy(
                src_ref=send_rows.at[target], dst_ref=recv_rows.at[source],
                send_sem=rows_sent.at[target], recv_sem=rows_here.at[sem],
                device_id=to, device_id_type=MESH),
            pltpu.make_async_remote_copy(
                src_ref=send_slot.at[target], dst_ref=recv_slot.at[source],
                send_sem=slot_sent.at[target], recv_sem=slot_here.at[sem],
                device_id=to, device_id_type=MESH),
        )

    @pl.loop(1, owners)
    def _(ahead):
        for copy in copies(lax.rem(me + ahead, owners), me, me):
            copy.start()

    recv_rows[me] = send_rows[me]
    recv_slot[me] = send_slot[me]

    @pl.loop(1, owners)
    def _(ahead):
        source = lax.rem(me + ahead, owners)
        for copy in copies(source, source, source):
            copy.wait_recv()

    @pl.loop(1, owners)
    def _(ahead):
        for copy in copies(lax.rem(me + ahead, owners), me, me):
            copy.wait_send()


def dispatch(x_in, x_grad, p_in, p_out, owner_row, slot_row):
    owners = lax.axis_size("blk")
    count, width = x_in.shape[0], p_in.shape[0]
    capacity = 4 * count // owners
    rows = (owners, capacity, 2 * width)
    slots = (owners, 1, LANES)
    return pl.pallas_call(
        functools.partial(dispatch_kernel, owners, capacity),
        out_shape=(jax.ShapeDtypeStruct(rows, BF16), jax.ShapeDtypeStruct(slots, jnp.int32)),
        in_specs=[VMEM_SPEC] * 6,
        out_specs=(VMEM_SPEC, VMEM_SPEC),
        scratch_shapes=[
            pltpu.VMEM((count, 2 * width), BF16),
            pltpu.VMEM(rows, BF16),
            pltpu.VMEM(slots, jnp.int32),
        ] + [pltpu.SemaphoreType.DMA((owners,))] * 4,
        compiler_params=pltpu.CompilerParams(collective_id=0, has_side_effects=True),
        name="dispatch",
    )(x_in, x_grad, p_in, p_out, owner_row, slot_row)


def prepare(recv_rows, recv_slot, turned, codes):
    owners, capacity, full = recv_rows.shape
    total = owners * capacity
    group = LANES // capacity
    rows = recv_rows[...].reshape(total, full)
    for part in range(total // LANES):
        span = slice(part * LANES, (part + 1) * LANES)
        turned[:, span] = rows[span].T
        code = recv_slot[part * group]
        for source in range(part * group + 1, (part + 1) * group):
            code = code + recv_slot[source]
        codes[:, span] = code


def query_group(step, recv_rows, turned, codes, flat, out):
    owners, capacity, full = recv_rows.shape
    width = full // 2
    row = lax.broadcasted_iota(jnp.int32, (width, full), 0)
    col = lax.broadcasted_iota(jnp.int32, (width, full), 1)
    left = col < width
    left_eye = jnp.where(row == col, 1.0, 0.0)
    right_eye = jnp.where(row + width == col, 1.0, 0.0)
    docs = range(DOC_GROUP)
    code = codes[...]
    counts, masked = [], []
    for doc in docs:
        hot = jnp.where(code == step * DOC_GROUP + doc + 1, 1.0, 0.0)
        counts.append(jnp.sum(hot, axis=1, keepdims=True))
        masked.append(turned[...] * hot.astype(BF16))
    rows = recv_rows[...].reshape(owners * capacity, full)
    half = DOC_GROUP // 2
    grams = [
        matmul(jnp.concatenate(masked[at:at + half], axis=0), rows) for at in (0, half)
    ]
    crossed, states = [], []
    for doc in docs:
        gram = grams[doc // half][doc % half * full:(doc % half + 1) * full]
        top, bottom = gram[:width], gram[width:]
        crossed.append(top)
        pair = []
        for outer in (top, pltpu.roll(bottom, width, 1)):
            damped = jnp.where(left, outer / (counts[doc] + 1.0), 0.0) + left_eye
            sums = jnp.sum(jnp.abs(damped), axis=1, keepdims=True)
            scale = 1.0 / jnp.max(sums, axis=0, keepdims=True)
            pair.append(left_eye - damped * scale + right_eye * scale)
        states.append(pair)
    for level in range(NEWTON_STEPS):
        for doc in docs:
            products = pair_product(states[doc], states[doc], False)
            states[doc] = [
                product + jnp.where(left, 0.0, state)
                for product, state in zip(products, states[doc])
            ]
    for doc in range(0, DOC_GROUP, 2):
        pair = (doc, doc + 1)
        tilted = pair_product(
            [states[d][0] for d in pair], [crossed[d] for d in pair], True)
        tilted = pair_product(tilted, [states[d][1] for d in pair], True)
        for d, value in zip(pair, tilted):
            flat[d * width:(d + 1) * width, :] = value

    near = lax.broadcasted_iota(jnp.int32, (DOC_GROUP, full), 1) < width
    for pair in range(width // 2):
        even = flat[pl.ds(2 * pair, DOC_GROUP, stride=width), :]
        odd = flat[pl.ds(2 * pair + 1, DOC_GROUP, stride=width), :]
        both = jnp.where(near, pltpu.roll(even, width, 1), odd)
        out[:, pair * full:(pair + 1) * full] = both.astype(BF16)


def query_scratch(recv_rows):
    owners, capacity, full = recv_rows.shape
    total = owners * capacity
    return [
        pltpu.VMEM((full, total), BF16),
        pltpu.VMEM((1, total), jnp.int32),
        pltpu.VMEM((DOC_GROUP * (full // 2), full), F32),
    ]


def queries_kernel(recv_rows, recv_slot, out, turned, codes, flat):
    prepare(recv_rows, recv_slot, turned, codes)

    @pl.loop(0, GROUPS)
    def _(step):
        query_group(step, recv_rows, turned, codes, flat, out.at[step])


def make_queries(recv_rows, recv_slot):
    width = recv_rows.shape[2] // 2
    return pl.pallas_call(
        queries_kernel,
        out_shape=jax.ShapeDtypeStruct((GROUPS, DOC_GROUP, width * width), BF16),
        in_specs=[VMEM_SPEC] * 2,
        out_specs=VMEM_SPEC,
        scratch_shapes=query_scratch(recv_rows),
        name="queries",
    )(recv_rows, recv_slot).reshape(DOC_DEV, width * width)


def score_into(out, index, block, train):
    out[index] = lax.dot_general(
        block[...], train[...], CONTRACT_LAST, preferred_element_type=F32
    ).astype(BF16)


def window_kernel(owners, queries, train, out, held, sent, here):
    me = lax.axis_index("blk")
    barrier = pltpu.get_barrier_semaphore()

    def peer(stop):
        return lax.rem(me + stop - LEAD + owners, owners)

    def source(stop):
        return lax.rem(me - stop + LEAD + owners, owners)

    def copy(stop):
        return pltpu.make_async_remote_copy(
            src_ref=queries, dst_ref=held.at[stop], send_sem=sent.at[stop],
            recv_sem=here.at[stop], device_id={"blk": peer(stop)}, device_id_type=MESH)

    others = [stop for stop in range(STOPS) if stop != LEAD]
    for stop in others:
        pl.semaphore_signal(
            barrier, inc=1, device_id={"blk": source(stop)}, device_id_type=MESH
        )
    pl.semaphore_wait(barrier, len(others))
    for stop in others:
        copy(stop).start()
    score_into(out, LEAD, queries, train)
    for stop in others:
        copy(stop).wait_recv()
        score_into(out, stop, held.at[stop], train)
    for stop in others:
        copy(stop).wait_send()


def grid_kernel(owners, recv_rows, recv_slot, train, out, turned, codes, flat, held,
                up_sent, down_sent, side_sent, twin_sent, here):
    lines = owners // 4
    me = lax.axis_index("blk")
    core = lax.rem(me, 2)
    side = lax.rem(me // 2, 2)
    line = me // 4
    twin = me + 1 - 2 * core
    across = me + 2 - 4 * side
    to_twin, to_across = 1 - 2 * core, 2 - 4 * side
    above, below = me + 4, me - 4
    has_up, has_down = line + 1 < lines, line > 0

    barrier = pltpu.get_barrier_semaphore()

    def greet(device):
        pl.semaphore_signal(barrier, inc=1, device_id={"blk": device}, device_id_type=MESH)

    greet(twin)
    greet(across)
    pl.when(has_up)(lambda: greet(above))
    pl.when(has_down)(lambda: greet(below))
    prepare(recv_rows, recv_slot, turned, codes)

    def wrapped(stop):
        return stop % owners if isinstance(stop, int) else lax.rem(stop + 3 * owners, owners)

    def wanted(stop):
        return wrapped(stop) < STOPS

    def either(first, second):
        return True if first is True or second is True else first | second

    def both(first, second):
        if first is True or second is True:
            return second if first is True else first
        return first & second

    def when(wish, act):
        if wish is True:
            act()
        elif wish is not False:
            pl.when(wish)(act)

    def reached(distance, way):
        if distance == 0:
            return True
        return line >= distance if way == 0 else line < lines - distance

    def place(stage, way, column):
        distance = stage - column
        if distance < 0 or (distance == 0 and way == 1):
            return None
        stop = LEAD - 4 * distance * (2 * way - 1)
        if column:
            stop = stop - to_across
        real = reached(distance, way)
        hands = []
        if column == 0:
            if way == 0:
                hands.append((both(real, has_up), 0, above, stop + 4))
            if way == 1 or distance == 0:
                hands.append((both(real, has_down), 1, below, stop - 4))
            sideways = either(wanted(stop + to_across), wanted(stop + to_across + to_twin))
            if distance == 0:
                sideways = True
            hands.append((both(real, sideways), 2, across, stop + to_across))
        else:
            real = both(real, either(wanted(stop), wanted(stop + to_twin)))
        hands.append((both(real, wanted(stop + to_twin)), 3, twin, stop + to_twin))
        twin_stop = stop - to_twin
        from_twin = both(reached(distance, way), wanted(twin_stop))
        hands = [(wish, sem, device, wrapped(theirs)) for wish, sem, device, theirs in hands]
        return wrapped(stop), real, hands, wrapped(twin_stop), from_twin

    sems = (up_sent, down_sent, side_sent, twin_sent)
    stages = []
    for stage in range(lines + 1):
        found = [place(stage, way, column) for column in range(2) for way in range(2)]
        stages.append([item for item in found if item is not None])

    def copy(group, mine, sem, device, theirs):
        return pltpu.make_async_remote_copy(
            src_ref=held.at[group, mine], dst_ref=held.at[group, theirs],
            send_sem=sems[sem].at[group, mine], recv_sem=here.at[group, theirs],
            device_id={"blk": device}, device_id_type=MESH)

    def arrive(group, mine):
        copy(group, mine, 3, twin, mine).wait_recv()

    def hand_on(group, item):
        for wish, sem, device, theirs in item[2]:
            when(wish, lambda: copy(group, item[0], sem, device, theirs).start())

    @pl.loop(0, GROUPS + lines)
    def _(step):
        @pl.when(step < GROUPS)
        def _():
            query_group(step, recv_rows, turned, codes, flat, held.at[step, LEAD])

            @pl.when(step == 0)
            def _():
                pl.semaphore_wait(barrier, 2 + has_up.astype(jnp.int32) + has_down.astype(jnp.int32))

            hand_on(step, stages[0][0])

        for stage in range(lines, 0, -1):
            group = step - stage

            @pl.when((group >= 0) & (group < GROUPS))
            def _():
                for item in stages[stage]:
                    when(item[1], lambda: arrive(group, item[0]))
                    hand_on(group, item)

        @pl.when(step >= lines)
        def _():
            group = step - lines
            for items in stages:
                for _, _, _, twin_stop, from_twin in items:
                    when(from_twin, lambda: arrive(group, twin_stop))
            block = held[group, :STOPS].reshape(STOPS * DOC_GROUP, train.shape[1])
            tile = lax.dot_general(block, train[...], CONTRACT_LAST, preferred_element_type=F32)
            out[group] = tile.astype(BF16).reshape(STOPS, DOC_GROUP, train.shape[0])

    @pl.loop(0, GROUPS)
    def _(group):
        for items in stages:
            for item in items:
                for wish, sem, device, theirs in item[2]:
                    when(wish, lambda: copy(group, item[0], sem, device, theirs).wait_send())


def influence_of(recv_rows, recv_slot, train):
    owners = lax.axis_size("blk")
    params = pltpu.CompilerParams(collective_id=1, has_side_effects=True)
    if owners % 4 == 0 and owners < 2 * STOPS:
        tiles = pl.pallas_call(
            functools.partial(grid_kernel, owners),
            out_shape=jax.ShapeDtypeStruct((GROUPS, STOPS, DOC_GROUP, train.shape[0]), BF16),
            in_specs=[VMEM_SPEC] * 3,
            out_specs=VMEM_SPEC,
            scratch_shapes=query_scratch(recv_rows)
            + [pltpu.VMEM((GROUPS, owners, DOC_GROUP, train.shape[1]), BF16)]
            + [pltpu.SemaphoreType.DMA((GROUPS, owners))] * 5,
            compiler_params=params,
            name="influence",
        )(recv_rows, recv_slot, train)
        return tiles.transpose(1, 0, 2, 3).reshape(STOPS, DOC_DEV, train.shape[0])
    queries = make_queries(recv_rows, recv_slot)
    return pl.pallas_call(
        functools.partial(window_kernel, owners),
        out_shape=jax.ShapeDtypeStruct((STOPS, DOC_DEV, train.shape[0]), BF16),
        in_specs=[VMEM_SPEC] * 2,
        out_specs=VMEM_SPEC,
        scratch_shapes=[pltpu.VMEM((STOPS,) + queries.shape, BF16)]
        + [pltpu.SemaphoreType.DMA((STOPS,))] * 2,
        compiler_params=params,
        name="influence",
    )(queries, train)


def local(query_inputs, query_grads, proj_in, proj_out, train_rows, token_owner, token_slot):
    recv_rows, recv_slot = dispatch(
        query_inputs, query_grads, proj_in.T, proj_out.T,
        token_owner.reshape(1, -1), token_slot.reshape(1, -1),
    )
    return influence_of(recv_rows, recv_slot, train_rows)


def solution(mesh):
    placed = (
        P(("groups", "blk"), None),
        P(("groups", "blk"), None),
        P(),
        P(),
        P(("groups", "blk"), None),
        P(("groups", "blk"), None),
        P(("groups", "blk")),
    )
    return jax.shard_map(
        local,
        mesh=mesh,
        in_specs=placed,
        out_specs=P(None, None, ("groups", "blk")),
        check_vma=False,
    )
```

```python
import functools

import jax
import jax.numpy as jnp
from jax import lax
from jax.experimental import pallas as pl
from jax.experimental.pallas import tpu as pltpu
from jax.sharding import PartitionSpec as P

DOC_DEV = 32
STOPS = 12
NEWTON_STEPS = 6
LEAD = 5
LANES = 128
DOC_GROUP = 8
GROUPS = DOC_DEV // DOC_GROUP
FIRST_STEPS = 2
MESH = pl.DeviceIdType.MESH
VMEM_SPEC = pl.BlockSpec(memory_space=pltpu.VMEM)
F32 = jnp.float32
BF16 = jnp.bfloat16
CONTRACT_LAST = (((1,), (1,)), ((), ()))


def matmul(left, right):
    return jnp.dot(left, right, preferred_element_type=F32)


def halves(value):
    high = value.astype(BF16)
    return high, (value - high.astype(F32)).astype(BF16)


def left_parts(value, right_half):
    width = value.shape[1] // 2
    high = value.astype(BF16).astype(F32)
    low = value - high
    if right_half:
        high = pltpu.roll(high, width, 1)
    else:
        low = pltpu.roll(low, width, 1)
    is_left = lax.broadcasted_iota(jnp.int32, value.shape, 1) < width
    parts = jnp.where(is_left, high, low).astype(BF16)
    return jnp.concatenate([parts, parts], axis=1)


def pair_product(lefts, rights, right_half):
    high, low = zip(*[halves(value) for value in rights])
    high, low = jnp.concatenate(high, axis=1), jnp.concatenate(low, axis=1)
    product = matmul(
        jnp.concatenate([left_parts(value, right_half) for value in lefts], axis=0),
        jnp.concatenate([high, high, low, low], axis=0),
    )
    rows, cols = lefts[0].shape
    return product[:rows, :cols], product[rows:, cols:]


def dispatch_kernel(owners, capacity, x_in, x_grad, p_in, p_out, owner_row, slot_row,
                    recv_rows, recv_slot, low, send_rows, send_slot,
                    rows_sent, rows_here, slot_sent, slot_here):
    me = lax.axis_index("blk")
    barrier = pltpu.get_barrier_semaphore()

    @pl.loop(1, owners)
    def _(ahead):
        pl.semaphore_signal(
            barrier, inc=1, device_id={"blk": lax.rem(me + ahead, owners)}, device_id_type=MESH
        )

    count = x_in.shape[0]
    width = p_in.shape[0]
    for at, values, weights in ((0, x_grad, p_out), (width, x_in, p_in)):
        low[:, at:at + width] = lax.dot_general(
            values[...], weights[...], CONTRACT_LAST, preferred_element_type=F32
        ).astype(BF16)
    token = lax.broadcasted_iota(jnp.int32, (count, count), 0)
    other = lax.broadcasted_iota(jnp.int32, (count, count), 1)
    earlier = jnp.where(token < other, 1.0, 0.0).astype(BF16)
    owner_id = lax.broadcasted_iota(jnp.int32, (owners, count), 0)
    owner_hot = jnp.where(owner_id == owner_row[...], 1.0, 0.0)
    before = matmul(owner_hot.astype(BF16), earlier)
    rank = jnp.sum(before * owner_hot, axis=0, keepdims=True).astype(jnp.int32)
    position = owner_row[...] * capacity + rank
    place = lax.broadcasted_iota(jnp.int32, (owners * capacity, count), 0)
    placed = jnp.where(place == position, 1.0, 0.0).astype(BF16)
    send_rows[...] = matmul(placed, low[...]).astype(BF16).reshape(send_rows.shape)
    coded = jnp.where(owner_id == owner_row[...], slot_row[...] + 1, 0).astype(F32).astype(BF16)
    lane = lax.broadcasted_iota(jnp.int32, (LANES, count), 0)
    shift = lax.rem(me, LANES // capacity) * capacity
    spread = jnp.where(lane == rank + shift, 1.0, 0.0).astype(BF16)
    codes = lax.dot_general(coded, spread, CONTRACT_LAST, preferred_element_type=F32)
    codes = codes.astype(jnp.int32)
    for owner in range(owners):
        send_slot[owner] = codes[owner:owner + 1]
    pl.semaphore_wait(barrier, owners - 1)

    def copies(target, source, sem):
        to = {"blk": target}
        return (
            pltpu.make_async_remote_copy(
                src_ref=send_rows.at[target], dst_ref=recv_rows.at[source],
                send_sem=rows_sent.at[target], recv_sem=rows_here.at[sem],
                device_id=to, device_id_type=MESH),
            pltpu.make_async_remote_copy(
                src_ref=send_slot.at[target], dst_ref=recv_slot.at[source],
                send_sem=slot_sent.at[target], recv_sem=slot_here.at[sem],
                device_id=to, device_id_type=MESH),
        )

    @pl.loop(1, owners)
    def _(ahead):
        for copy in copies(lax.rem(me + ahead, owners), me, me):
            copy.start()

    recv_rows[me] = send_rows[me]
    recv_slot[me] = send_slot[me]

    @pl.loop(1, owners)
    def _(ahead):
        source = lax.rem(me + ahead, owners)
        for copy in copies(source, source, source):
            copy.wait_recv()

    @pl.loop(1, owners)
    def _(ahead):
        for copy in copies(lax.rem(me + ahead, owners), me, me):
            copy.wait_send()


def dispatch(x_in, x_grad, p_in, p_out, owner_row, slot_row):
    owners = lax.axis_size("blk")
    count, width = x_in.shape[0], p_in.shape[0]
    capacity = 4 * count // owners
    rows = (owners, capacity, 2 * width)
    slots = (owners, 1, LANES)
    return pl.pallas_call(
        functools.partial(dispatch_kernel, owners, capacity),
        out_shape=(jax.ShapeDtypeStruct(rows, BF16), jax.ShapeDtypeStruct(slots, jnp.int32)),
        in_specs=[VMEM_SPEC] * 6,
        out_specs=(VMEM_SPEC, VMEM_SPEC),
        scratch_shapes=[
            pltpu.VMEM((count, 2 * width), BF16),
            pltpu.VMEM(rows, BF16),
            pltpu.VMEM(slots, jnp.int32),
        ] + [pltpu.SemaphoreType.DMA((owners,))] * 4,
        compiler_params=pltpu.CompilerParams(collective_id=0, has_side_effects=True),
        name="dispatch",
    )(x_in, x_grad, p_in, p_out, owner_row, slot_row)


def prepare(recv_rows, recv_slot, turned, codes):
    owners, capacity, full = recv_rows.shape
    total = owners * capacity
    group = LANES // capacity
    rows = recv_rows[...].reshape(total, full)
    for part in range(total // LANES):
        span = slice(part * LANES, (part + 1) * LANES)
        turned[:, span] = rows[span].T
        code = recv_slot[part * group]
        for source in range(part * group + 1, (part + 1) * group):
            code = code + recv_slot[source]
        codes[:, span] = code


def start_group(step, recv_rows, turned, codes, state):
    owners, capacity, full = recv_rows.shape
    width = full // 2
    row = lax.broadcasted_iota(jnp.int32, (width, full), 0)
    col = lax.broadcasted_iota(jnp.int32, (width, full), 1)
    left = col < width
    left_eye = jnp.where(row == col, 1.0, 0.0)
    right_eye = jnp.where(row + width == col, 1.0, 0.0)
    docs = range(DOC_GROUP)
    code = codes[...]
    counts, masked = [], []
    for doc in docs:
        hot = jnp.where(code == step * DOC_GROUP + doc + 1, 1.0, 0.0)
        counts.append(jnp.sum(hot, axis=1, keepdims=True))
        masked.append(turned[...] * hot.astype(BF16))
    rows = recv_rows[...].reshape(owners * capacity, full)
    half = DOC_GROUP // 2
    grams = [
        matmul(jnp.concatenate(masked[at:at + half], axis=0), rows) for at in (0, half)
    ]
    crossed, states = [], []
    for doc in docs:
        gram = grams[doc // half][doc % half * full:(doc % half + 1) * full]
        top, bottom = gram[:width], gram[width:]
        crossed.append(top)
        pair = []
        for outer in (top, pltpu.roll(bottom, width, 1)):
            damped = jnp.where(left, outer / (counts[doc] + 1.0), 0.0) + left_eye
            sums = jnp.sum(jnp.abs(damped), axis=1, keepdims=True)
            scale = 1.0 / jnp.max(sums, axis=0, keepdims=True)
            pair.append(left_eye - damped * scale + right_eye * scale)
        states.append(pair)
    for doc, pair in enumerate(newton_steps(states, left, FIRST_STEPS)):
        state[doc, 0], state[doc, 1], state[doc, 2] = pair[0], pair[1], crossed[doc]


def newton_steps(states, left, steps):
    states = list(states)
    for level in range(steps):
        for doc in range(DOC_GROUP):
            products = pair_product(states[doc], states[doc], False)
            states[doc] = [
                product + jnp.where(left, 0.0, value)
                for product, value in zip(products, states[doc])
            ]
    return states


def finish_group(state, flat, out):
    width, full = state.shape[2:]
    left = lax.broadcasted_iota(jnp.int32, (width, full), 1) < width
    states = [[state[doc, 0], state[doc, 1]] for doc in range(DOC_GROUP)]
    states = newton_steps(states, left, NEWTON_STEPS - FIRST_STEPS)
    for doc in range(0, DOC_GROUP, 2):
        pair = (doc, doc + 1)
        tilted = pair_product([states[d][0] for d in pair], [state[d, 2] for d in pair], True)
        tilted = pair_product(tilted, [states[d][1] for d in pair], True)
        for d, value in zip(pair, tilted):
            flat[d * width:(d + 1) * width, :] = value

    near = lax.broadcasted_iota(jnp.int32, (DOC_GROUP, full), 1) < width
    for pair in range(width // 2):
        even = flat[pl.ds(2 * pair, DOC_GROUP, stride=width), :]
        odd = flat[pl.ds(2 * pair + 1, DOC_GROUP, stride=width), :]
        both = jnp.where(near, pltpu.roll(even, width, 1), odd)
        out[:, pair * full:(pair + 1) * full] = both.astype(BF16)


def query_scratch(recv_rows):
    owners, capacity, full = recv_rows.shape
    total = owners * capacity
    return [
        pltpu.VMEM((full, total), BF16),
        pltpu.VMEM((1, total), jnp.int32),
        pltpu.VMEM((DOC_GROUP, 3, full // 2, full), F32),
        pltpu.VMEM((DOC_GROUP * (full // 2), full), F32),
    ]


def queries_kernel(recv_rows, recv_slot, out, turned, codes, state, flat):
    prepare(recv_rows, recv_slot, turned, codes)

    @pl.loop(0, GROUPS)
    def _(step):
        start_group(step, recv_rows, turned, codes, state)
        finish_group(state, flat, out.at[step])


def make_queries(recv_rows, recv_slot):
    width = recv_rows.shape[2] // 2
    return pl.pallas_call(
        queries_kernel,
        out_shape=jax.ShapeDtypeStruct((GROUPS, DOC_GROUP, width * width), BF16),
        in_specs=[VMEM_SPEC] * 2,
        out_specs=VMEM_SPEC,
        scratch_shapes=query_scratch(recv_rows),
        name="queries",
    )(recv_rows, recv_slot).reshape(DOC_DEV, width * width)


def score_into(out, index, block, train):
    out[index] = lax.dot_general(
        block[...], train[...], CONTRACT_LAST, preferred_element_type=F32
    ).astype(BF16)


def window_kernel(owners, queries, train, out, held, sent, here):
    me = lax.axis_index("blk")
    barrier = pltpu.get_barrier_semaphore()

    def peer(stop):
        return lax.rem(me + stop - LEAD + owners, owners)

    def source(stop):
        return lax.rem(me - stop + LEAD + owners, owners)

    def copy(stop):
        return pltpu.make_async_remote_copy(
            src_ref=queries, dst_ref=held.at[stop], send_sem=sent.at[stop],
            recv_sem=here.at[stop], device_id={"blk": peer(stop)}, device_id_type=MESH)

    others = [stop for stop in range(STOPS) if stop != LEAD]
    for stop in others:
        pl.semaphore_signal(
            barrier, inc=1, device_id={"blk": source(stop)}, device_id_type=MESH
        )
    pl.semaphore_wait(barrier, len(others))
    for stop in others:
        copy(stop).start()
    score_into(out, LEAD, queries, train)
    for stop in others:
        copy(stop).wait_recv()
        score_into(out, stop, held.at[stop], train)
    for stop in others:
        copy(stop).wait_send()


def grid_kernel(owners, recv_rows, recv_slot, train, out, turned, codes, state, flat, held,
                up_sent, down_sent, side_sent, twin_sent, here):
    lines = owners // 4
    me = lax.axis_index("blk")
    core = lax.rem(me, 2)
    side = lax.rem(me // 2, 2)
    line = me // 4
    twin = me + 1 - 2 * core
    across = me + 2 - 4 * side
    to_twin, to_across = 1 - 2 * core, 2 - 4 * side
    above, below = me + 4, me - 4
    has_up, has_down = line + 1 < lines, line > 0

    barrier = pltpu.get_barrier_semaphore()

    def greet(device):
        pl.semaphore_signal(barrier, inc=1, device_id={"blk": device}, device_id_type=MESH)

    greet(twin)
    greet(across)
    pl.when(has_up)(lambda: greet(above))
    pl.when(has_down)(lambda: greet(below))
    prepare(recv_rows, recv_slot, turned, codes)

    def wrapped(stop):
        return stop % owners if isinstance(stop, int) else lax.rem(stop + 3 * owners, owners)

    def wanted(stop):
        return wrapped(stop) < STOPS

    def either(first, second):
        return True if first is True or second is True else first | second

    def both(first, second):
        if first is True or second is True:
            return second if first is True else first
        return first & second

    def when(wish, act):
        if wish is True:
            act()
        elif wish is not False:
            pl.when(wish)(act)

    def reached(distance, way):
        if distance == 0:
            return True
        return line >= distance if way == 0 else line < lines - distance

    def place(stage, way, column):
        distance = stage - column
        if distance < 0 or (distance == 0 and way == 1):
            return None
        stop = LEAD - 4 * distance * (2 * way - 1)
        if column:
            stop = stop - to_across
        real = reached(distance, way)
        hands = []
        if column == 0:
            if way == 0:
                hands.append((both(real, has_up), 0, above, stop + 4))
            if way == 1 or distance == 0:
                hands.append((both(real, has_down), 1, below, stop - 4))
            sideways = either(wanted(stop + to_across), wanted(stop + to_across + to_twin))
            if distance == 0:
                sideways = True
            hands.append((both(real, sideways), 2, across, stop + to_across))
        else:
            real = both(real, either(wanted(stop), wanted(stop + to_twin)))
        hands.append((both(real, wanted(stop + to_twin)), 3, twin, stop + to_twin))
        twin_stop = stop - to_twin
        from_twin = both(reached(distance, way), wanted(twin_stop))
        hands = [(wish, sem, device, wrapped(theirs)) for wish, sem, device, theirs in hands]
        return wrapped(stop), real, hands, wrapped(twin_stop), from_twin

    sems = (up_sent, down_sent, side_sent, twin_sent)
    stages = []
    for stage in range(lines + 1):
        found = [place(stage, way, column) for column in range(2) for way in range(2)]
        stages.append([item for item in found if item is not None])

    def copy(group, mine, sem, device, theirs):
        return pltpu.make_async_remote_copy(
            src_ref=held.at[group, mine], dst_ref=held.at[group, theirs],
            send_sem=sems[sem].at[group, mine], recv_sem=here.at[group, theirs],
            device_id={"blk": device}, device_id_type=MESH)

    def arrive(group, mine):
        copy(group, mine, 3, twin, mine).wait_recv()

    def hand_on(group, item):
        for wish, sem, device, theirs in item[2]:
            when(wish, lambda: copy(group, item[0], sem, device, theirs).start())

    def relay(step, stages_now):
        for stage in stages_now:
            group = step - (stage + 1) // 2

            @pl.when((group >= 0) & (group < GROUPS))
            def _():
                for item in stages[stage]:
                    when(item[1], lambda: arrive(group, item[0]))
                    hand_on(group, item)

    last = (lines + 1) // 2 + 1

    @pl.loop(0, GROUPS + last)
    def _(step):
        @pl.when(step < GROUPS)
        def _():
            start_group(step, recv_rows, turned, codes, state)

            @pl.when(step == 0)
            def _():
                pl.semaphore_wait(barrier, 2 + has_up.astype(jnp.int32) + has_down.astype(jnp.int32))

        relay(step, [stage for stage in range(lines, 0, -1) if stage % 2 == 1])

        @pl.when(step >= last)
        def _():
            group = step - last
            for items in stages:
                for _, _, _, twin_stop, from_twin in items:
                    when(from_twin, lambda: arrive(group, twin_stop))
            block = held[group, :STOPS].reshape(STOPS * DOC_GROUP, train.shape[1])
            tile = lax.dot_general(block, train[...], CONTRACT_LAST, preferred_element_type=F32)
            out[group] = tile.astype(BF16).reshape(STOPS, DOC_GROUP, train.shape[0])

        @pl.when(step < GROUPS)
        def _():
            finish_group(state, flat, held.at[step, LEAD])

            hand_on(step, stages[0][0])

        relay(step, [stage for stage in range(lines, 0, -1) if stage % 2 == 0])

    @pl.loop(0, GROUPS)
    def _(group):
        for items in stages:
            for item in items:
                for wish, sem, device, theirs in item[2]:
                    when(wish, lambda: copy(group, item[0], sem, device, theirs).wait_send())


def influence_of(recv_rows, recv_slot, train):
    owners = lax.axis_size("blk")
    params = pltpu.CompilerParams(collective_id=1, has_side_effects=True)
    if owners % 4 == 0 and owners < 2 * STOPS:
        tiles = pl.pallas_call(
            functools.partial(grid_kernel, owners),
            out_shape=jax.ShapeDtypeStruct((GROUPS, STOPS, DOC_GROUP, train.shape[0]), BF16),
            in_specs=[VMEM_SPEC] * 3,
            out_specs=VMEM_SPEC,
            scratch_shapes=query_scratch(recv_rows)
            + [pltpu.VMEM((GROUPS, owners, DOC_GROUP, train.shape[1]), BF16)]
            + [pltpu.SemaphoreType.DMA((GROUPS, owners))] * 5,
            compiler_params=params,
            name="influence",
        )(recv_rows, recv_slot, train)
        return tiles.transpose(1, 0, 2, 3).reshape(STOPS, DOC_DEV, train.shape[0])
    queries = make_queries(recv_rows, recv_slot)
    return pl.pallas_call(
        functools.partial(window_kernel, owners),
        out_shape=jax.ShapeDtypeStruct((STOPS, DOC_DEV, train.shape[0]), BF16),
        in_specs=[VMEM_SPEC] * 2,
        out_specs=VMEM_SPEC,
        scratch_shapes=[pltpu.VMEM((STOPS,) + queries.shape, BF16)]
        + [pltpu.SemaphoreType.DMA((STOPS,))] * 2,
        compiler_params=params,
        name="influence",
    )(queries, train)


def local(query_inputs, query_grads, proj_in, proj_out, train_rows, token_owner, token_slot):
    recv_rows, recv_slot = dispatch(
        query_inputs, query_grads, proj_in.T, proj_out.T,
        token_owner.reshape(1, -1), token_slot.reshape(1, -1),
    )
    return influence_of(recv_rows, recv_slot, train_rows)


def solution(mesh):
    placed = (
        P(("groups", "blk"), None),
        P(("groups", "blk"), None),
        P(),
        P(),
        P(("groups", "blk"), None),
        P(("groups", "blk"), None),
        P(("groups", "blk")),
    )
    return jax.shard_map(
        local,
        mesh=mesh,
        in_specs=placed,
        out_specs=P(None, None, ("groups", "blk")),
        check_vma=False,
    )
```

```python
import functools

import jax
import jax.numpy as jnp
from jax import lax
from jax.experimental import pallas as pl
from jax.experimental.pallas import tpu as pltpu
from jax.sharding import PartitionSpec as P

DOC_DEV = 32
STOPS = 12
NEWTON_STEPS = 6
LEAD = 5
LANES = 128
DOC_GROUP = 8
GROUPS = DOC_DEV // DOC_GROUP
MESH = pl.DeviceIdType.MESH
VMEM_SPEC = pl.BlockSpec(memory_space=pltpu.VMEM)
F32 = jnp.float32
BF16 = jnp.bfloat16
CONTRACT_LAST = (((1,), (1,)), ((), ()))


def matmul(left, right):
    return jnp.dot(left, right, preferred_element_type=F32)


def halves(value):
    high = value.astype(BF16)
    return high, (value - high.astype(F32)).astype(BF16)


def left_parts(value, right_half):
    width = value.shape[1] // 2
    high = value.astype(BF16).astype(F32)
    low = value - high
    if right_half:
        high = pltpu.roll(high, width, 1)
    else:
        low = pltpu.roll(low, width, 1)
    is_left = lax.broadcasted_iota(jnp.int32, value.shape, 1) < width
    parts = jnp.where(is_left, high, low).astype(BF16)
    return jnp.concatenate([parts, parts], axis=1)


def pair_product(lefts, rights, right_half):
    high, low = zip(*[halves(value) for value in rights])
    high, low = jnp.concatenate(high, axis=1), jnp.concatenate(low, axis=1)
    product = matmul(
        jnp.concatenate([left_parts(value, right_half) for value in lefts], axis=0),
        jnp.concatenate([high, high, low, low], axis=0),
    )
    rows, cols = lefts[0].shape
    return product[:rows, :cols], product[rows:, cols:]


def dispatch_kernel(owners, capacity, far_in, far_grad, p_in, p_out, owner_row, slot_row,
                    recv_rows, recv_slot, x_in, x_grad, fetched, low, send_rows, send_slot,
                    rows_sent, rows_here, slot_sent, slot_here):
    me = lax.axis_index("blk")
    fetch_grad = pltpu.make_async_copy(far_grad, x_grad, fetched.at[0])
    fetch_in = pltpu.make_async_copy(far_in, x_in, fetched.at[1])
    fetch_grad.start()
    fetch_in.start()
    barrier = pltpu.get_barrier_semaphore()

    @pl.loop(1, owners)
    def _(ahead):
        pl.semaphore_signal(
            barrier, inc=1, device_id={"blk": lax.rem(me + ahead, owners)}, device_id_type=MESH
        )

    count = x_in.shape[0]
    width = p_in.shape[0]
    token = lax.broadcasted_iota(jnp.int32, (count, count), 0)
    other = lax.broadcasted_iota(jnp.int32, (count, count), 1)
    earlier = jnp.where(token < other, 1.0, 0.0).astype(BF16)
    owner_id = lax.broadcasted_iota(jnp.int32, (owners, count), 0)
    owner_hot = jnp.where(owner_id == owner_row[...], 1.0, 0.0)
    before = matmul(owner_hot.astype(BF16), earlier)
    rank = jnp.sum(before * owner_hot, axis=0, keepdims=True).astype(jnp.int32)
    position = owner_row[...] * capacity + rank
    place = lax.broadcasted_iota(jnp.int32, (owners * capacity, count), 0)
    placed = jnp.where(place == position, 1.0, 0.0).astype(BF16)
    for at, values, weights, fetch in (
        (0, x_grad, p_out, fetch_grad), (width, x_in, p_in, fetch_in)
    ):
        fetch.wait()
        low[:, at:at + width] = lax.dot_general(
            values[...], weights[...], CONTRACT_LAST, preferred_element_type=F32
        ).astype(BF16)
    send_rows[...] = matmul(placed, low[...]).astype(BF16).reshape(send_rows.shape)
    coded = jnp.where(owner_id == owner_row[...], slot_row[...] + 1, 0).astype(F32).astype(BF16)
    lane = lax.broadcasted_iota(jnp.int32, (LANES, count), 0)
    shift = lax.rem(me, LANES // capacity) * capacity
    spread = jnp.where(lane == rank + shift, 1.0, 0.0).astype(BF16)
    codes = lax.dot_general(coded, spread, CONTRACT_LAST, preferred_element_type=F32)
    codes = codes.astype(jnp.int32)
    for owner in range(owners):
        send_slot[owner] = codes[owner:owner + 1]
    pl.semaphore_wait(barrier, owners - 1)

    def copies(target, source, sem):
        to = {"blk": target}
        return (
            pltpu.make_async_remote_copy(
                src_ref=send_rows.at[target], dst_ref=recv_rows.at[source],
                send_sem=rows_sent.at[target], recv_sem=rows_here.at[sem],
                device_id=to, device_id_type=MESH),
            pltpu.make_async_remote_copy(
                src_ref=send_slot.at[target], dst_ref=recv_slot.at[source],
                send_sem=slot_sent.at[target], recv_sem=slot_here.at[sem],
                device_id=to, device_id_type=MESH),
        )

    @pl.loop(1, owners)
    def _(ahead):
        for copy in copies(lax.rem(me + ahead, owners), me, me):
            copy.start()

    recv_rows[me] = send_rows[me]
    recv_slot[me] = send_slot[me]

    @pl.loop(1, owners)
    def _(ahead):
        source = lax.rem(me + ahead, owners)
        for copy in copies(source, source, source):
            copy.wait_recv()

    @pl.loop(1, owners)
    def _(ahead):
        for copy in copies(lax.rem(me + ahead, owners), me, me):
            copy.wait_send()


def dispatch(x_in, x_grad, p_in, p_out, owner_row, slot_row):
    owners = lax.axis_size("blk")
    count, width = x_in.shape[0], p_in.shape[0]
    capacity = 4 * count // owners
    rows = (owners, capacity, 2 * width)
    slots = (owners, 1, LANES)
    return pl.pallas_call(
        functools.partial(dispatch_kernel, owners, capacity),
        out_shape=(jax.ShapeDtypeStruct(rows, BF16), jax.ShapeDtypeStruct(slots, jnp.int32)),
        in_specs=[pl.BlockSpec(memory_space=pl.ANY)] * 2 + [VMEM_SPEC] * 4,
        out_specs=(VMEM_SPEC, VMEM_SPEC),
        scratch_shapes=[
            pltpu.VMEM(x_in.shape, BF16),
            pltpu.VMEM(x_in.shape, BF16),
            pltpu.SemaphoreType.DMA((2,)),
            pltpu.VMEM((count, 2 * width), BF16),
            pltpu.VMEM(rows, BF16),
            pltpu.VMEM(slots, jnp.int32),
        ] + [pltpu.SemaphoreType.DMA((owners,))] * 4,
        compiler_params=pltpu.CompilerParams(collective_id=0, has_side_effects=True),
        name="dispatch",
    )(x_in, x_grad, p_in, p_out, owner_row, slot_row)


def prepare(recv_rows, recv_slot, turned, codes):
    owners, capacity, full = recv_rows.shape
    total = owners * capacity
    group = LANES // capacity
    rows = recv_rows[...].reshape(total, full)
    for part in range(total // LANES):
        span = slice(part * LANES, (part + 1) * LANES)
        turned[:, span] = rows[span].T
        code = recv_slot[part * group]
        for source in range(part * group + 1, (part + 1) * group):
            code = code + recv_slot[source]
        codes[:, span] = code


def query_group(step, recv_rows, turned, codes, flat, out):
    owners, capacity, full = recv_rows.shape
    width = full // 2
    row = lax.broadcasted_iota(jnp.int32, (width, full), 0)
    col = lax.broadcasted_iota(jnp.int32, (width, full), 1)
    left = col < width
    left_eye = jnp.where(row == col, 1.0, 0.0)
    right_eye = jnp.where(row + width == col, 1.0, 0.0)
    docs = range(DOC_GROUP)
    code = codes[...]
    counts, masked = [], []
    for doc in docs:
        hot = jnp.where(code == step * DOC_GROUP + doc + 1, 1.0, 0.0)
        counts.append(jnp.sum(hot, axis=1, keepdims=True))
        masked.append(turned[...] * hot.astype(BF16))
    rows = recv_rows[...].reshape(owners * capacity, full)
    half = DOC_GROUP // 2
    grams = [
        matmul(jnp.concatenate(masked[at:at + half], axis=0), rows) for at in (0, half)
    ]
    crossed, states = [], []
    for doc in docs:
        gram = grams[doc // half][doc % half * full:(doc % half + 1) * full]
        top, bottom = gram[:width], gram[width:]
        crossed.append(top)
        pair = []
        for outer in (top, pltpu.roll(bottom, width, 1)):
            damped = jnp.where(left, outer / (counts[doc] + 1.0), 0.0) + left_eye
            sums = jnp.sum(jnp.abs(damped), axis=1, keepdims=True)
            scale = 1.0 / jnp.max(sums, axis=0, keepdims=True)
            pair.append(left_eye - damped * scale + right_eye * scale)
        states.append(pair)
    for level in range(NEWTON_STEPS):
        for doc in docs:
            products = pair_product(states[doc], states[doc], False)
            states[doc] = [
                product + jnp.where(left, 0.0, state)
                for product, state in zip(products, states[doc])
            ]
    for doc in range(0, DOC_GROUP, 2):
        pair = (doc, doc + 1)
        tilted = pair_product(
            [states[d][0] for d in pair], [crossed[d] for d in pair], True)
        tilted = pair_product(tilted, [states[d][1] for d in pair], True)
        for d, value in zip(pair, tilted):
            flat[d * width:(d + 1) * width, :] = value

    near = lax.broadcasted_iota(jnp.int32, (DOC_GROUP, full), 1) < width
    for pair in range(width // 2):
        even = flat[pl.ds(2 * pair, DOC_GROUP, stride=width), :]
        odd = flat[pl.ds(2 * pair + 1, DOC_GROUP, stride=width), :]
        both = jnp.where(near, pltpu.roll(even, width, 1), odd)
        out[:, pair * full:(pair + 1) * full] = both.astype(BF16)


def query_scratch(recv_rows):
    owners, capacity, full = recv_rows.shape
    total = owners * capacity
    return [
        pltpu.VMEM((full, total), BF16),
        pltpu.VMEM((1, total), jnp.int32),
        pltpu.VMEM((DOC_GROUP * (full // 2), full), F32),
    ]


def queries_kernel(recv_rows, recv_slot, out, turned, codes, flat):
    prepare(recv_rows, recv_slot, turned, codes)

    @pl.loop(0, GROUPS)
    def _(step):
        query_group(step, recv_rows, turned, codes, flat, out.at[step])


def make_queries(recv_rows, recv_slot):
    width = recv_rows.shape[2] // 2
    return pl.pallas_call(
        queries_kernel,
        out_shape=jax.ShapeDtypeStruct((GROUPS, DOC_GROUP, width * width), BF16),
        in_specs=[VMEM_SPEC] * 2,
        out_specs=VMEM_SPEC,
        scratch_shapes=query_scratch(recv_rows),
        name="queries",
    )(recv_rows, recv_slot).reshape(DOC_DEV, width * width)


def score_into(out, index, block, train):
    out[index] = lax.dot_general(
        block[...], train[...], CONTRACT_LAST, preferred_element_type=F32
    ).astype(BF16)


def window_kernel(owners, queries, train, out, held, sent, here):
    me = lax.axis_index("blk")
    barrier = pltpu.get_barrier_semaphore()

    def peer(stop):
        return lax.rem(me + stop - LEAD + owners, owners)

    def source(stop):
        return lax.rem(me - stop + LEAD + owners, owners)

    def copy(stop):
        return pltpu.make_async_remote_copy(
            src_ref=queries, dst_ref=held.at[stop], send_sem=sent.at[stop],
            recv_sem=here.at[stop], device_id={"blk": peer(stop)}, device_id_type=MESH)

    others = [stop for stop in range(STOPS) if stop != LEAD]
    for stop in others:
        pl.semaphore_signal(
            barrier, inc=1, device_id={"blk": source(stop)}, device_id_type=MESH
        )
    pl.semaphore_wait(barrier, len(others))
    for stop in others:
        copy(stop).start()
    score_into(out, LEAD, queries, train)
    for stop in others:
        copy(stop).wait_recv()
        score_into(out, stop, held.at[stop], train)
    for stop in others:
        copy(stop).wait_send()


def grid_kernel(owners, recv_rows, recv_slot, train_far, out, turned, codes, flat, train, fetched, held,
                up_sent, down_sent, side_sent, twin_sent, here):
    lines = owners // 4
    me = lax.axis_index("blk")
    core = lax.rem(me, 2)
    side = lax.rem(me // 2, 2)
    line = me // 4
    twin = me + 1 - 2 * core
    across = me + 2 - 4 * side
    to_twin, to_across = 1 - 2 * core, 2 - 4 * side
    above, below = me + 4, me - 4
    has_up, has_down = line + 1 < lines, line > 0

    barrier = pltpu.get_barrier_semaphore()

    def greet(device):
        pl.semaphore_signal(barrier, inc=1, device_id={"blk": device}, device_id_type=MESH)

    greet(twin)
    greet(across)
    pl.when(has_up)(lambda: greet(above))
    pl.when(has_down)(lambda: greet(below))
    fetch = pltpu.make_async_copy(train_far, train, fetched)
    fetch.start()
    prepare(recv_rows, recv_slot, turned, codes)

    def wrapped(stop):
        return stop % owners if isinstance(stop, int) else lax.rem(stop + 3 * owners, owners)

    def wanted(stop):
        return wrapped(stop) < STOPS

    def either(first, second):
        return True if first is True or second is True else first | second

    def both(first, second):
        if first is True or second is True:
            return second if first is True else first
        return first & second

    def when(wish, act):
        if wish is True:
            act()
        elif wish is not False:
            pl.when(wish)(act)

    def reached(distance, way):
        if distance == 0:
            return True
        return line >= distance if way == 0 else line < lines - distance

    def place(stage, way, column):
        distance = stage - column
        if distance < 0 or (distance == 0 and way == 1):
            return None
        stop = LEAD - 4 * distance * (2 * way - 1)
        if column:
            stop = stop - to_across
        real = reached(distance, way)
        hands = []
        if column == 0:
            if way == 0:
                hands.append((both(real, has_up), 0, above, stop + 4))
            if way == 1 or distance == 0:
                hands.append((both(real, has_down), 1, below, stop - 4))
            sideways = either(wanted(stop + to_across), wanted(stop + to_across + to_twin))
            if distance == 0:
                sideways = True
            hands.append((both(real, sideways), 2, across, stop + to_across))
        else:
            real = both(real, either(wanted(stop), wanted(stop + to_twin)))
        hands.append((both(real, wanted(stop + to_twin)), 3, twin, stop + to_twin))
        twin_stop = stop - to_twin
        from_twin = both(reached(distance, way), wanted(twin_stop))
        hands = [(wish, sem, device, wrapped(theirs)) for wish, sem, device, theirs in hands]
        return wrapped(stop), real, hands, wrapped(twin_stop), from_twin

    sems = (up_sent, down_sent, side_sent, twin_sent)
    stages = []
    for stage in range(lines + 1):
        found = [place(stage, way, column) for column in range(2) for way in range(2)]
        stages.append([item for item in found if item is not None])

    def copy(group, mine, sem, device, theirs):
        return pltpu.make_async_remote_copy(
            src_ref=held.at[group, mine], dst_ref=held.at[group, theirs],
            send_sem=sems[sem].at[group, mine], recv_sem=here.at[group, theirs],
            device_id={"blk": device}, device_id_type=MESH)

    def arrive(group, mine):
        copy(group, mine, 3, twin, mine).wait_recv()

    def hand_on(group, item):
        for wish, sem, device, theirs in item[2]:
            when(wish, lambda: copy(group, item[0], sem, device, theirs).start())

    @pl.loop(0, GROUPS + lines)
    def _(step):
        @pl.when(step < GROUPS)
        def _():
            query_group(step, recv_rows, turned, codes, flat, held.at[step, LEAD])

            @pl.when(step == 0)
            def _():
                pl.semaphore_wait(barrier, 2 + has_up.astype(jnp.int32) + has_down.astype(jnp.int32))

            hand_on(step, stages[0][0])

        for stage in range(lines, 0, -1):
            group = step - stage

            @pl.when((group >= 0) & (group < GROUPS))
            def _():
                for item in stages[stage]:
                    when(item[1], lambda: arrive(group, item[0]))
                    hand_on(group, item)

        @pl.when(step >= lines)
        def _():
            group = step - lines
            for items in stages:
                for _, _, _, twin_stop, from_twin in items:
                    when(from_twin, lambda: arrive(group, twin_stop))
            pl.when(group == 0)(fetch.wait)
            block = held[group, :STOPS].reshape(STOPS * DOC_GROUP, train.shape[1])
            tile = lax.dot_general(block, train[...], CONTRACT_LAST, preferred_element_type=F32)
            out[group] = tile.astype(BF16).reshape(STOPS, DOC_GROUP, train.shape[0])

    @pl.loop(0, GROUPS)
    def _(group):
        for items in stages:
            for item in items:
                for wish, sem, device, theirs in item[2]:
                    when(wish, lambda: copy(group, item[0], sem, device, theirs).wait_send())


def influence_of(recv_rows, recv_slot, train):
    owners = lax.axis_size("blk")
    params = pltpu.CompilerParams(collective_id=1, has_side_effects=True)
    if owners % 4 == 0 and owners < 2 * STOPS:
        tiles = pl.pallas_call(
            functools.partial(grid_kernel, owners),
            out_shape=jax.ShapeDtypeStruct((GROUPS, STOPS, DOC_GROUP, train.shape[0]), BF16),
            in_specs=[VMEM_SPEC, VMEM_SPEC, pl.BlockSpec(memory_space=pl.ANY)],
            out_specs=VMEM_SPEC,
            scratch_shapes=query_scratch(recv_rows)
            + [pltpu.VMEM(train.shape, BF16), pltpu.SemaphoreType.DMA]
            + [pltpu.VMEM((GROUPS, owners, DOC_GROUP, train.shape[1]), BF16)]
            + [pltpu.SemaphoreType.DMA((GROUPS, owners))] * 5,
            compiler_params=params,
            name="influence",
        )(recv_rows, recv_slot, train)
        return tiles.transpose(1, 0, 2, 3).reshape(STOPS, DOC_DEV, train.shape[0])
    queries = make_queries(recv_rows, recv_slot)
    return pl.pallas_call(
        functools.partial(window_kernel, owners),
        out_shape=jax.ShapeDtypeStruct((STOPS, DOC_DEV, train.shape[0]), BF16),
        in_specs=[VMEM_SPEC] * 2,
        out_specs=VMEM_SPEC,
        scratch_shapes=[pltpu.VMEM((STOPS,) + queries.shape, BF16)]
        + [pltpu.SemaphoreType.DMA((STOPS,))] * 2,
        compiler_params=params,
        name="influence",
    )(queries, train)


def local(query_inputs, query_grads, proj_in, proj_out, train_rows, token_owner, token_slot):
    recv_rows, recv_slot = dispatch(
        query_inputs, query_grads, proj_in.T, proj_out.T,
        token_owner.reshape(1, -1), token_slot.reshape(1, -1),
    )
    return influence_of(recv_rows, recv_slot, train_rows)


def solution(mesh):
    placed = (
        P(("groups", "blk"), None),
        P(("groups", "blk"), None),
        P(),
        P(),
        P(("groups", "blk"), None),
        P(("groups", "blk"), None),
        P(("groups", "blk")),
    )
    return jax.shard_map(
        local,
        mesh=mesh,
        in_specs=placed,
        out_specs=P(None, None, ("groups", "blk")),
        check_vma=False,
    )
```

```python
import functools

import jax
import jax.numpy as jnp
from jax import lax
from jax.experimental import pallas as pl
from jax.experimental.pallas import tpu as pltpu
from jax.sharding import PartitionSpec as P

DOC_DEV = 32
STOPS = 12
NEWTON_STEPS = 6
LEAD = 5
LANES = 128
DOC_GROUP = 4
GROUPS = DOC_DEV // DOC_GROUP
MESH = pl.DeviceIdType.MESH
VMEM_SPEC = pl.BlockSpec(memory_space=pltpu.VMEM)
F32 = jnp.float32
BF16 = jnp.bfloat16
CONTRACT_LAST = (((1,), (1,)), ((), ()))


def matmul(left, right):
    return jnp.dot(left, right, preferred_element_type=F32)


def halves(value):
    high = value.astype(BF16)
    return high, (value - high.astype(F32)).astype(BF16)


def left_parts(value, right_half):
    width = value.shape[1] // 2
    high = value.astype(BF16).astype(F32)
    low = value - high
    if right_half:
        high = pltpu.roll(high, width, 1)
    else:
        low = pltpu.roll(low, width, 1)
    is_left = lax.broadcasted_iota(jnp.int32, value.shape, 1) < width
    parts = jnp.where(is_left, high, low).astype(BF16)
    return jnp.concatenate([parts, parts], axis=1)


def pair_product(lefts, rights, right_half):
    high, low = zip(*[halves(value) for value in rights])
    high, low = jnp.concatenate(high, axis=1), jnp.concatenate(low, axis=1)
    product = matmul(
        jnp.concatenate([left_parts(value, right_half) for value in lefts], axis=0),
        jnp.concatenate([high, high, low, low], axis=0),
    )
    rows, cols = lefts[0].shape
    return product[:rows, :cols], product[rows:, cols:]


def dispatch_kernel(owners, capacity, x_in, x_grad, p_in, p_out, owner_row, slot_row,
                    recv_rows, recv_slot, low, send_rows, send_slot,
                    rows_sent, rows_here, slot_sent, slot_here):
    me = lax.axis_index("blk")
    barrier = pltpu.get_barrier_semaphore()

    @pl.loop(1, owners)
    def _(ahead):
        pl.semaphore_signal(
            barrier, inc=1, device_id={"blk": lax.rem(me + ahead, owners)}, device_id_type=MESH
        )

    count = x_in.shape[0]
    width = p_in.shape[0]
    for at, values, weights in ((0, x_grad, p_out), (width, x_in, p_in)):
        low[:, at:at + width] = lax.dot_general(
            values[...], weights[...], CONTRACT_LAST, preferred_element_type=F32
        ).astype(BF16)
    token = lax.broadcasted_iota(jnp.int32, (count, count), 0)
    other = lax.broadcasted_iota(jnp.int32, (count, count), 1)
    earlier = jnp.where(token < other, 1.0, 0.0).astype(BF16)
    owner_id = lax.broadcasted_iota(jnp.int32, (owners, count), 0)
    owner_hot = jnp.where(owner_id == owner_row[...], 1.0, 0.0)
    before = matmul(owner_hot.astype(BF16), earlier)
    rank = jnp.sum(before * owner_hot, axis=0, keepdims=True).astype(jnp.int32)
    position = owner_row[...] * capacity + rank
    place = lax.broadcasted_iota(jnp.int32, (owners * capacity, count), 0)
    placed = jnp.where(place == position, 1.0, 0.0).astype(BF16)
    send_rows[...] = matmul(placed, low[...]).astype(BF16).reshape(send_rows.shape)
    coded = jnp.where(owner_id == owner_row[...], slot_row[...] + 1, 0).astype(F32).astype(BF16)
    lane = lax.broadcasted_iota(jnp.int32, (LANES, count), 0)
    shift = lax.rem(me, LANES // capacity) * capacity
    spread = jnp.where(lane == rank + shift, 1.0, 0.0).astype(BF16)
    codes = lax.dot_general(coded, spread, CONTRACT_LAST, preferred_element_type=F32)
    codes = codes.astype(jnp.int32)
    for owner in range(owners):
        send_slot[owner] = codes[owner:owner + 1]
    pl.semaphore_wait(barrier, owners - 1)

    def copies(target, source, sem):
        to = {"blk": target}
        return (
            pltpu.make_async_remote_copy(
                src_ref=send_rows.at[target], dst_ref=recv_rows.at[source],
                send_sem=rows_sent.at[target], recv_sem=rows_here.at[sem],
                device_id=to, device_id_type=MESH),
            pltpu.make_async_remote_copy(
                src_ref=send_slot.at[target], dst_ref=recv_slot.at[source],
                send_sem=slot_sent.at[target], recv_sem=slot_here.at[sem],
                device_id=to, device_id_type=MESH),
        )

    @pl.loop(1, owners)
    def _(ahead):
        for copy in copies(lax.rem(me + ahead, owners), me, me):
            copy.start()

    recv_rows[me] = send_rows[me]
    recv_slot[me] = send_slot[me]

    @pl.loop(1, owners)
    def _(ahead):
        source = lax.rem(me + ahead, owners)
        for copy in copies(source, source, source):
            copy.wait_recv()

    @pl.loop(1, owners)
    def _(ahead):
        for copy in copies(lax.rem(me + ahead, owners), me, me):
            copy.wait_send()


def dispatch(x_in, x_grad, p_in, p_out, owner_row, slot_row):
    owners = lax.axis_size("blk")
    count, width = x_in.shape[0], p_in.shape[0]
    capacity = 4 * count // owners
    rows = (owners, capacity, 2 * width)
    slots = (owners, 1, LANES)
    return pl.pallas_call(
        functools.partial(dispatch_kernel, owners, capacity),
        out_shape=(jax.ShapeDtypeStruct(rows, BF16), jax.ShapeDtypeStruct(slots, jnp.int32)),
        in_specs=[VMEM_SPEC] * 6,
        out_specs=(VMEM_SPEC, VMEM_SPEC),
        scratch_shapes=[
            pltpu.VMEM((count, 2 * width), BF16),
            pltpu.VMEM(rows, BF16),
            pltpu.VMEM(slots, jnp.int32),
        ] + [pltpu.SemaphoreType.DMA((owners,))] * 4,
        compiler_params=pltpu.CompilerParams(collective_id=0, has_side_effects=True),
        name="dispatch",
    )(x_in, x_grad, p_in, p_out, owner_row, slot_row)


def prepare(recv_rows, recv_slot, turned, codes):
    owners, capacity, full = recv_rows.shape
    total = owners * capacity
    group = LANES // capacity
    rows = recv_rows[...].reshape(total, full)
    for part in range(total // LANES):
        span = slice(part * LANES, (part + 1) * LANES)
        turned[:, span] = rows[span].T
        code = recv_slot[part * group]
        for source in range(part * group + 1, (part + 1) * group):
            code = code + recv_slot[source]
        codes[:, span] = code


def query_group(step, recv_rows, turned, codes, flat, out):
    owners, capacity, full = recv_rows.shape
    width = full // 2
    row = lax.broadcasted_iota(jnp.int32, (width, full), 0)
    col = lax.broadcasted_iota(jnp.int32, (width, full), 1)
    left = col < width
    left_eye = jnp.where(row == col, 1.0, 0.0)
    right_eye = jnp.where(row + width == col, 1.0, 0.0)
    docs = range(DOC_GROUP)
    code = codes[...]
    counts, masked = [], []
    for doc in docs:
        hot = jnp.where(code == step * DOC_GROUP + doc + 1, 1.0, 0.0)
        counts.append(jnp.sum(hot, axis=1, keepdims=True))
        masked.append(turned[...] * hot.astype(BF16))
    rows = recv_rows[...].reshape(owners * capacity, full)
    half = DOC_GROUP // 2
    grams = [
        matmul(jnp.concatenate(masked[at:at + half], axis=0), rows) for at in (0, half)
    ]
    crossed, states = [], []
    for doc in docs:
        gram = grams[doc // half][doc % half * full:(doc % half + 1) * full]
        top, bottom = gram[:width], gram[width:]
        crossed.append(top)
        pair = []
        for outer in (top, pltpu.roll(bottom, width, 1)):
            damped = jnp.where(left, outer / (counts[doc] + 1.0), 0.0) + left_eye
            sums = jnp.sum(jnp.abs(damped), axis=1, keepdims=True)
            scale = 1.0 / jnp.max(sums, axis=0, keepdims=True)
            pair.append(left_eye - damped * scale + right_eye * scale)
        states.append(pair)
    for level in range(NEWTON_STEPS):
        for doc in docs:
            products = pair_product(states[doc], states[doc], False)
            states[doc] = [
                product + jnp.where(left, 0.0, state)
                for product, state in zip(products, states[doc])
            ]
    for doc in range(0, DOC_GROUP, 2):
        pair = (doc, doc + 1)
        tilted = pair_product(
            [states[d][0] for d in pair], [crossed[d] for d in pair], True)
        tilted = pair_product(tilted, [states[d][1] for d in pair], True)
        for d, value in zip(pair, tilted):
            flat[d * width:(d + 1) * width, :] = value

    near = lax.broadcasted_iota(jnp.int32, (DOC_GROUP, full), 1) < width
    for pair in range(width // 2):
        even = flat[pl.ds(2 * pair, DOC_GROUP, stride=width), :]
        odd = flat[pl.ds(2 * pair + 1, DOC_GROUP, stride=width), :]
        both = jnp.where(near, pltpu.roll(even, width, 1), odd)
        out[:, pair * full:(pair + 1) * full] = both.astype(BF16)


def query_scratch(recv_rows):
    owners, capacity, full = recv_rows.shape
    total = owners * capacity
    return [
        pltpu.VMEM((full, total), BF16),
        pltpu.VMEM((1, total), jnp.int32),
        pltpu.VMEM((DOC_GROUP * (full // 2), full), F32),
    ]


def queries_kernel(recv_rows, recv_slot, out, turned, codes, flat):
    prepare(recv_rows, recv_slot, turned, codes)

    @pl.loop(0, GROUPS)
    def _(step):
        query_group(step, recv_rows, turned, codes, flat, out.at[step])


def make_queries(recv_rows, recv_slot):
    width = recv_rows.shape[2] // 2
    return pl.pallas_call(
        queries_kernel,
        out_shape=jax.ShapeDtypeStruct((GROUPS, DOC_GROUP, width * width), BF16),
        in_specs=[VMEM_SPEC] * 2,
        out_specs=VMEM_SPEC,
        scratch_shapes=query_scratch(recv_rows),
        name="queries",
    )(recv_rows, recv_slot).reshape(DOC_DEV, width * width)


def score_into(out, index, block, train):
    out[index] = lax.dot_general(
        block[...], train[...], CONTRACT_LAST, preferred_element_type=F32
    ).astype(BF16)


def window_kernel(owners, queries, train, out, held, sent, here):
    me = lax.axis_index("blk")
    barrier = pltpu.get_barrier_semaphore()

    def peer(stop):
        return lax.rem(me + stop - LEAD + owners, owners)

    def source(stop):
        return lax.rem(me - stop + LEAD + owners, owners)

    def copy(stop):
        return pltpu.make_async_remote_copy(
            src_ref=queries, dst_ref=held.at[stop], send_sem=sent.at[stop],
            recv_sem=here.at[stop], device_id={"blk": peer(stop)}, device_id_type=MESH)

    others = [stop for stop in range(STOPS) if stop != LEAD]
    for stop in others:
        pl.semaphore_signal(
            barrier, inc=1, device_id={"blk": source(stop)}, device_id_type=MESH
        )
    pl.semaphore_wait(barrier, len(others))
    for stop in others:
        copy(stop).start()
    score_into(out, LEAD, queries, train)
    for stop in others:
        copy(stop).wait_recv()
        score_into(out, stop, held.at[stop], train)
    for stop in others:
        copy(stop).wait_send()


def grid_kernel(owners, recv_rows, recv_slot, train, out, turned, codes, flat, held,
                up_sent, down_sent, side_sent, twin_sent, here):
    lines = owners // 4
    me = lax.axis_index("blk")
    core = lax.rem(me, 2)
    side = lax.rem(me // 2, 2)
    line = me // 4
    twin = me + 1 - 2 * core
    across = me + 2 - 4 * side
    to_twin, to_across = 1 - 2 * core, 2 - 4 * side
    above, below = me + 4, me - 4
    has_up, has_down = line + 1 < lines, line > 0

    barrier = pltpu.get_barrier_semaphore()

    def greet(device):
        pl.semaphore_signal(barrier, inc=1, device_id={"blk": device}, device_id_type=MESH)

    greet(twin)
    greet(across)
    pl.when(has_up)(lambda: greet(above))
    pl.when(has_down)(lambda: greet(below))
    prepare(recv_rows, recv_slot, turned, codes)

    def wrapped(stop):
        return stop % owners if isinstance(stop, int) else lax.rem(stop + 3 * owners, owners)

    def wanted(stop):
        return wrapped(stop) < STOPS

    def either(first, second):
        return True if first is True or second is True else first | second

    def both(first, second):
        if first is True or second is True:
            return second if first is True else first
        return first & second

    def when(wish, act):
        if wish is True:
            act()
        elif wish is not False:
            pl.when(wish)(act)

    def reached(distance, way):
        if distance == 0:
            return True
        return line >= distance if way == 0 else line < lines - distance

    def place(stage, way, column):
        distance = stage - column
        if distance < 0 or (distance == 0 and way == 1):
            return None
        stop = LEAD - 4 * distance * (2 * way - 1)
        if column:
            stop = stop - to_across
        real = reached(distance, way)
        hands = []
        if column == 0:
            if way == 0:
                hands.append((both(real, has_up), 0, above, stop + 4))
            if way == 1 or distance == 0:
                hands.append((both(real, has_down), 1, below, stop - 4))
            sideways = either(wanted(stop + to_across), wanted(stop + to_across + to_twin))
            if distance == 0:
                sideways = True
            hands.append((both(real, sideways), 2, across, stop + to_across))
        else:
            real = both(real, either(wanted(stop), wanted(stop + to_twin)))
        hands.append((both(real, wanted(stop + to_twin)), 3, twin, stop + to_twin))
        twin_stop = stop - to_twin
        from_twin = both(reached(distance, way), wanted(twin_stop))
        hands = [(wish, sem, device, wrapped(theirs)) for wish, sem, device, theirs in hands]
        return wrapped(stop), real, hands, wrapped(twin_stop), from_twin

    sems = (up_sent, down_sent, side_sent, twin_sent)
    stages = []
    for stage in range(lines + 1):
        found = [place(stage, way, column) for column in range(2) for way in range(2)]
        stages.append([item for item in found if item is not None])

    def copy(group, mine, sem, device, theirs):
        return pltpu.make_async_remote_copy(
            src_ref=held.at[group, mine], dst_ref=held.at[group, theirs],
            send_sem=sems[sem].at[group, mine], recv_sem=here.at[group, theirs],
            device_id={"blk": device}, device_id_type=MESH)

    def arrive(group, mine):
        copy(group, mine, 3, twin, mine).wait_recv()

    def hand_on(group, item):
        for wish, sem, device, theirs in item[2]:
            when(wish, lambda: copy(group, item[0], sem, device, theirs).start())

    @pl.loop(0, GROUPS + lines)
    def _(step):
        @pl.when(step < GROUPS)
        def _():
            query_group(step, recv_rows, turned, codes, flat, held.at[step, LEAD])

            @pl.when(step == 0)
            def _():
                pl.semaphore_wait(barrier, 2 + has_up.astype(jnp.int32) + has_down.astype(jnp.int32))

            hand_on(step, stages[0][0])

        for stage in range(lines, 0, -1):
            group = step - stage

            @pl.when((group >= 0) & (group < GROUPS))
            def _():
                for item in stages[stage]:
                    when(item[1], lambda: arrive(group, item[0]))
                    hand_on(group, item)

        @pl.when(step >= lines)
        def _():
            group = step - lines
            for items in stages:
                for _, _, _, twin_stop, from_twin in items:
                    when(from_twin, lambda: arrive(group, twin_stop))
            block = held[group, :STOPS].reshape(STOPS * DOC_GROUP, train.shape[1])
            tile = lax.dot_general(block, train[...], CONTRACT_LAST, preferred_element_type=F32)
            out[group] = tile.astype(BF16).reshape(STOPS, DOC_GROUP, train.shape[0])

    @pl.loop(0, GROUPS)
    def _(group):
        for items in stages:
            for item in items:
                for wish, sem, device, theirs in item[2]:
                    when(wish, lambda: copy(group, item[0], sem, device, theirs).wait_send())


def influence_of(recv_rows, recv_slot, train):
    owners = lax.axis_size("blk")
    params = pltpu.CompilerParams(collective_id=1, has_side_effects=True)
    if owners % 4 == 0 and owners < 2 * STOPS:
        tiles = pl.pallas_call(
            functools.partial(grid_kernel, owners),
            out_shape=jax.ShapeDtypeStruct((GROUPS, STOPS, DOC_GROUP, train.shape[0]), BF16),
            in_specs=[VMEM_SPEC] * 3,
            out_specs=VMEM_SPEC,
            scratch_shapes=query_scratch(recv_rows)
            + [pltpu.VMEM((GROUPS, owners, DOC_GROUP, train.shape[1]), BF16)]
            + [pltpu.SemaphoreType.DMA((GROUPS, owners))] * 5,
            compiler_params=params,
            name="influence",
        )(recv_rows, recv_slot, train)
        return tiles.transpose(1, 0, 2, 3).reshape(STOPS, DOC_DEV, train.shape[0])
    queries = make_queries(recv_rows, recv_slot)
    return pl.pallas_call(
        functools.partial(window_kernel, owners),
        out_shape=jax.ShapeDtypeStruct((STOPS, DOC_DEV, train.shape[0]), BF16),
        in_specs=[VMEM_SPEC] * 2,
        out_specs=VMEM_SPEC,
        scratch_shapes=[pltpu.VMEM((STOPS,) + queries.shape, BF16)]
        + [pltpu.SemaphoreType.DMA((STOPS,))] * 2,
        compiler_params=params,
        name="influence",
    )(queries, train)


def local(query_inputs, query_grads, proj_in, proj_out, train_rows, token_owner, token_slot):
    recv_rows, recv_slot = dispatch(
        query_inputs, query_grads, proj_in.T, proj_out.T,
        token_owner.reshape(1, -1), token_slot.reshape(1, -1),
    )
    return influence_of(recv_rows, recv_slot, train_rows)


def solution(mesh):
    placed = (
        P(("groups", "blk"), None),
        P(("groups", "blk"), None),
        P(),
        P(),
        P(("groups", "blk"), None),
        P(("groups", "blk"), None),
        P(("groups", "blk")),
    )
    return jax.shard_map(
        local,
        mesh=mesh,
        in_specs=placed,
        out_specs=P(None, None, ("groups", "blk")),
        check_vma=False,
    )
```
